256 devices in a mesh: dp: 32 (over z, y), cuts: 8 (over x, core).
Axes of the slice: x: 4, y: 4, z: 8, core: 2. Of those that a mesh axis runs over, the one named last changes fastest.
Arguments:
- tokens: bfloat16 [512, 6144], P('dp', 'cuts'), may hold values from -6 to 6
- out_grad: bfloat16 [512, 6144], P('dp', 'cuts'), may hold values from -6 to 6
- gate_values: float32 [512, 2], P('dp'), may hold values from 0.2 to 1
- routing: int32 [512, 2], P('dp'), may hold values from 0 to 7, all different within a row; in each aligned block of 16 rows (0 to 15, 16 to 31, ...) at most 8 rows name the same one
- gate_weight: bfloat16 [32, 6144, 2816], P('dp', None, 'cuts'), may hold values from -0.078125 to 0.078125
- up_weight: bfloat16 [32, 6144, 2816], P('dp', None, 'cuts'), may hold values from -0.078125 to 0.078125
- down_weight: bfloat16 [32, 2816, 6144], P('dp', 'cuts'), may hold values from -0.0546875 to 0.0546875
Outputs:
- mixed: bfloat16 [512, 6144], P('dp', 'cuts')
- token_grad: bfloat16 [512, 6144], P('dp', 'cuts')
The draws below stay inside these ranges and needn't reach their ends.
Inputs may be any that keep to these rules, and one draw needn't show every extreme that they name: `routing`: each row names 2 different experts; in each aligned block of 16 rows (the rows of one index of dp) no expert is named by more than 8 rows, and in some block one expert is named by exactly 8 rows.
All inputs are finite; a program needn't handle non-finite values.
Results may differ from the reference program's by a relative error of at most 0.019.
Values may be sent and summed in bfloat16 or wider, within the bound.
No kernel may reach another device: no remote copies, remote signals or barrier semaphores. Data moves between devices by JAX's collectives and lax.ppermute only.
A program may use at most 64 MiB of HBM per device.

```python
import math
import jax
import jax.numpy as jnp
import numpy as np
from jax import lax

D = 6144
E = 8
TOPK = 2
FF = 11264
TOK = 16
CAP = 8
TOKENS = 512
SUBS = 4
FFQ = 2816
HID = 352
SLOTS = 256
N_DP = 32


def steps_of(key, dims, cuts, smallest, largest):
    gain, own = 1.0, jax.random.fold_in(key, 6)
    for axis_at, blocks in cuts:
        heights = jnp.exp(jax.random.uniform(jax.random.fold_in(own, axis_at), (blocks,), jnp.float32, smallest / len(cuts), largest / len(cuts)))
        gain = gain * jnp.repeat(heights, dims[axis_at] // blocks).reshape([-1 if axis == axis_at else 1 for axis in range(len(dims))])
    return gain


def shared_out(key, own, number, rows, count, top, reach, lean):
    sequence = jax.random.permutation(key, count)
    packed, common = portions_of(count, rows * top, reach, lean, True), portions_of(count, rows * top, reach, lean, False)
    places = jnp.arange(count)

    def named(sizes, offset_by):
        used = int((sizes > 0).sum())
        fixed = max(1, used // 4)
        shifted = fixed + (places - fixed + offset_by * (used - fixed)) % max(1, count - fixed)
        return jnp.zeros((count,), jnp.int32).at[sequence[jnp.where(places < fixed, places, shifted)]].set(jnp.asarray(sizes, jnp.int32))

    sizes = jnp.where(number % 4 == 0, named(packed, number // 4), named(common, number - number // 4 - 1))
    mixed = jax.random.permutation(jax.random.fold_in(own, 3), count)
    donor, receiver = mixed[0:count // 2 * 2:2], mixed[1:count // 2 * 2:2]
    margin = jnp.minimum(sizes[donor] - 1, reach - sizes[receiver]) // 2
    margin = jnp.where((donor == sequence[0]) | (receiver == sequence[0]) | (sizes[receiver] == 0), 0, jnp.maximum(margin, 0))
    shifted = jax.random.randint(jax.random.fold_in(own, 4), (count // 2,), 0, 1 << 20) % (margin + 1)
    sizes = sizes.at[donor].add(-shifted).at[receiver].add(shifted)
    labels = jnp.searchsorted(jnp.cumsum(sizes), jnp.arange(rows * top), side="right").astype(jnp.int32)
    table = labels.reshape(top, rows).T
    table = table[jax.random.permutation(jax.random.fold_in(own, 1), rows)]
    offset_by = jax.random.randint(jax.random.fold_in(own, 2), (rows, 1), 0, top)
    return jnp.take_along_axis(table, (jnp.arange(top)[None, :] + offset_by) % top, axis=1)


def portions_of(amount, total, limit, skew, full):
    portions = [(1 << 20) // math.isqrt(standing ** skew) + 1 for standing in range(1, amount + 1)]
    largest = limit if full else min(limit, max(-(-total // amount), total * portions[0] // sum(portions)))
    least = 1 if total - largest >= amount - 1 else 0
    given, surplus = [largest] + [least] * (amount - 1), total - largest - least * (amount - 1)
    while surplus > 0:
        candidates = [i for i in range(1, amount) if given[i] < largest] or [i for i in range(1, amount) if given[i] < limit]
        mass, budget = sum([portions[i] for i in candidates]), surplus
        for i in candidates:
            more = min(limit - given[i], max(1, budget * portions[i] // mass), surplus)
            given[i] = given[i] + more
            surplus = surplus - more
    return np.array(given)


def gaussian(rng, dims, scale, limit, pieces=(), kind=jnp.bfloat16):
    drawn = jax.random.normal(rng, dims, jnp.float32) * scale
    if len(pieces) > 0:
        drawn = steps_of(rng, dims, pieces, -0.22, 0.18) * drawn
    return jnp.clip(drawn, min=-limit, max=limit).astype(kind)


def setup_inputs(seed: int = 0) -> dict:
    arg_keys = jax.random.split(jax.random.key(seed), 8)
    tokens = gaussian(arg_keys[0], (TOKENS, D), 1.0, 6.0, ((0, 32), (1, 8)))
    out_grad = gaussian(arg_keys[1], (TOKENS, D), 1.0, 6.0, ((0, 32), (1, 8)))
    gate_values = jnp.clip(0.2 + 0.8 * jax.random.uniform(arg_keys[2], (TOKENS, TOPK), jnp.float32) ** steps_of(arg_keys[2], (TOKENS, TOPK), ((0, 32),), -0.2, 0.2), 0.2, 1.0)
    routing_keys = jax.random.split(jax.random.fold_in(arg_keys[3], 1), TOKENS // TOK)
    routing_turns = jax.random.permutation(jax.random.fold_in(arg_keys[3], 3), TOKENS // TOK)
    routing = jax.vmap(lambda own, number: shared_out(jax.random.fold_in(arg_keys[3], 2), own, number, TOK, E, TOPK, CAP, 2))(routing_keys, routing_turns).reshape((TOKENS, TOPK))
    gate_weight = gaussian(arg_keys[4], (N_DP, D, FFQ), D ** -0.5, 0.078125, ((0, 32), (2, 8)))
    up_weight = gaussian(arg_keys[5], (N_DP, D, FFQ), D ** -0.5, 0.078125, ((0, 32), (2, 8)))
    down_weight = gaussian(arg_keys[6], (N_DP, FFQ, D), FF ** -0.5, 0.0546875, ((0, 32), (1, 8)))
    return {"tokens": tokens, "out_grad": out_grad, "gate_values": gate_values, "routing": routing, "gate_weight": gate_weight, "up_weight": up_weight, "down_weight": down_weight}


def expert_weights(gate_weight, up_weight, down_weight, expert):
    wg = jnp.concatenate([gate_weight[expert * SUBS + s] for s in range(SUBS)], axis=1)
    wu = jnp.concatenate([up_weight[expert * SUBS + s] for s in range(SUBS)], axis=1)
    w2 = jnp.concatenate([down_weight[expert * SUBS + s] for s in range(SUBS)], axis=0)
    return wg, wu, w2


def reference(tokens, out_grad, gate_values, routing, gate_weight, up_weight, down_weight):
    pair_count = TOKENS * TOPK
    experts = routing.reshape(-1)
    pairs_x = jnp.concatenate([jnp.repeat(tokens, TOPK, axis=0), jnp.zeros((1, D), jnp.bfloat16)], axis=0)
    scaled = (gate_values[:, :, None] * out_grad[:, None, :].astype(jnp.float32)).astype(jnp.bfloat16)
    scaled = jnp.concatenate([scaled.reshape(pair_count, D), jnp.zeros((1, D), jnp.bfloat16)], axis=0)
    y_pairs = jnp.zeros((pair_count + 1, D), jnp.float32)
    dx_pairs = jnp.zeros((pair_count + 1, D), jnp.float32)
    blocks = FF // HID
    contract = (((1,), (1,)), ((), ()))
    for expert in range(E):
        index = jnp.nonzero(experts == expert, size=SLOTS, fill_value=pair_count)[0].astype(jnp.int32)
        rows_x = pairs_x[index]
        rows_dy = scaled[index]
        wg, wu, w2 = expert_weights(gate_weight, up_weight, down_weight, expert)
        gate_pre = jnp.dot(rows_x, wg, preferred_element_type=jnp.float32)
        up_pre = jnp.dot(rows_x, wu, preferred_element_type=jnp.float32)
        sigma = jax.nn.sigmoid(gate_pre)
        silu = gate_pre * sigma
        hidden = (silu * up_pre).astype(jnp.bfloat16)
        hid_grad = lax.dot_general(rows_dy, w2, contract, preferred_element_type=jnp.float32)
        gate_grad = (hid_grad * up_pre * sigma * (1.0 + gate_pre * (1.0 - sigma))).astype(jnp.bfloat16)
        up_grad = (hid_grad * silu).astype(jnp.bfloat16)

        def block_term(carry, block):
            start = block * HID
            hid_block = lax.dynamic_slice_in_dim(hidden, start, HID, 1)
            down_block = lax.dynamic_slice_in_dim(w2, start, HID, 0)
            out_part = jnp.dot(hid_block, down_block, preferred_element_type=jnp.float32).astype(jnp.bfloat16)
            gg_block = lax.dynamic_slice_in_dim(gate_grad, start, HID, 1)
            ug_block = lax.dynamic_slice_in_dim(up_grad, start, HID, 1)
            wg_block = lax.dynamic_slice_in_dim(wg, start, HID, 1)
            wu_block = lax.dynamic_slice_in_dim(wu, start, HID, 1)
            in_part = lax.dot_general(gg_block, wg_block, contract, preferred_element_type=jnp.float32)
            in_part = in_part + lax.dot_general(ug_block, wu_block, contract, preferred_element_type=jnp.float32)
            in_part = in_part.astype(jnp.bfloat16)
            out_part, in_part = lax.optimization_barrier((out_part, in_part))
            return (carry[0] + out_part.astype(jnp.float32), carry[1] + in_part.astype(jnp.float32)), None

        start_sums = (jnp.zeros((SLOTS, D), jnp.float32), jnp.zeros((SLOTS, D), jnp.float32))
        sums, unused = lax.scan(block_term, start_sums, jnp.arange(blocks, dtype=jnp.int32))
        y_pairs = y_pairs.at[index].add(sums[0])
        dx_pairs = dx_pairs.at[index].add(sums[1])
    mixed = jnp.sum(y_pairs[:pair_count].reshape(TOKENS, TOPK, D) * gate_values[:, :, None], axis=1)
    token_grad = jnp.sum(dx_pairs[:pair_count].reshape(TOKENS, TOPK, D), axis=1)
    return mixed.astype(jnp.bfloat16), token_grad.astype(jnp.bfloat16)
```

```python
import functools

import jax
import jax.numpy as jnp
from jax import lax
from jax.experimental import pallas as pl
from jax.experimental.pallas import tpu as pltpu
from jax.sharding import PartitionSpec as P

E = 8
NY = 4
NX = 4
CAP = 8
BF = jnp.bfloat16
F32 = jnp.float32
NT = (((1,), (1,)), ((), ()))
VMEM_LIMIT = 24 << 20


def swap_z(v):
    groups = [[z * NY + y for z in range(E)] for y in range(NY)]
    return lax.all_to_all(v, "dp", 0, 0, axis_index_groups=groups, tiled=True)


def to_y(v, d):
    perm = [(z * NY + y, z * NY + (y + d) % NY) for z in range(E) for y in range(NY)]
    return lax.ppermute(v, "dp", perm)


def to_x(v, d):
    perm = [(x * 2 + c, (x + d) % NX * 2 + c) for x in range(NX) for c in range(2)]
    return lax.ppermute(v, "cuts", perm)


def to_core(v):
    return lax.ppermute(v, "cuts", [(i, i ^ 1) for i in range(2 * NX)])


def slots_of(routing, gate_values):
    hit = routing[:, :, None] == jnp.arange(E, dtype=jnp.int32)
    chosen = jnp.any(hit, axis=1)
    gates = jnp.sum(jnp.where(hit, gate_values[:, :, None], 0.0), axis=1)
    rows = routing.shape[0]
    below = jnp.arange(rows)[:, None] > jnp.arange(rows)[None, :]
    position = jnp.sum(
        jnp.where(below[:, :, None] & chosen[None, :, :], 1, 0), axis=1
    )
    slot = position[:, :, None] == jnp.arange(CAP, dtype=jnp.int32)
    select = chosen[:, :, None] & slot
    weight = jnp.where(select, gates[:, :, None], 0.0)
    return select.reshape(rows, E * CAP), weight.reshape(rows, E * CAP)


def first_gather(a, b):
    order = (1, 3, 2)
    ra, rb = {0: a}, {0: b}
    for d in order:
        ra[d] = to_y(a, d)
        rb[d] = to_x(b, d)
    return [ra[d] for d in range(4)], [rb[d] for d in range(4)]


def second_gather(a, b):
    order = (1, 3, 2)
    ra, rb = {0: a}, {0: b}
    for d in order:
        ra[d] = to_x(a, d)
        rb[d] = to_y(b, d)
    return [ra[d] for d in range(4)], [rb[d] for d in range(4)]


def add(*parts):
    total = parts[0].astype(F32)
    for p in parts[1:]:
        total = total + p.astype(F32)
    return total.astype(BF)


def first_scatter(sa, sb):
    ra, rb = [sa[0]], [sb[0]]
    for d in (1, 3, 2):
        ra.append(to_x(sa[d], d))
        rb.append(to_y(sb[d], -d))
    return add(*ra), add(*rb)


def second_scatter(ta, tb):
    ra, rb = [ta[0]], [tb[0]]
    for d in (1, 3, 2):
        ra.append(to_y(ta[d], -d))
        rb.append(to_x(tb[d], d))
    return add(*ra), add(*rb)


def column(off_ref, i, width):
    return pl.ds(pl.multiple_of(off_ref[i] * width, 128), width)


NP = 2 * (NX + NY)


def load_rows(pieces, rows):
    half = rows.shape[1] // 2
    step = half // NY
    for dc in range(2):
        base = dc * (NX + NY)
        for k in range(NX):
            rows[dc * NX + k, :half] = pieces[base + k][...].reshape(half, -1)
            for j in range(NY):
                at = half + j * step
                rows[dc * NX + k, at : at + step] = pieces[base + NX + j][k]


def store_rows(pieces, rows):
    half = rows.shape[1] // 2
    step = half // NY
    for dc in range(2):
        base = dc * (NX + NY)
        for k in range(NX):
            pieces[base + k][...] = rows[dc * NX + k, :half].reshape(NY, step, -1)
            for j in range(NY):
                at = half + j * step
                pieces[base + NX + j][k] = rows[dc * NX + k, at : at + step]


def forward_kernel(width, off_in, off_out, *refs):
    pieces, (wg, wu, w2), outs = refs[:NP], refs[NP : NP + 3], refs[NP + 3 :]
    out_pieces, (gate, up, rows) = outs[:NP], outs[NP:]
    load_rows(pieces, rows)
    gate[...] = jnp.zeros_like(gate)
    up[...] = jnp.zeros_like(up)

    @pl.loop(0, 2 * NX)
    def _(i):
        cols = column(off_in, i, width)
        r = rows[i]
        gate[...] += lax.dot_general(r, wg[:, cols], NT, preferred_element_type=F32)
        up[...] += lax.dot_general(r, wu[:, cols], NT, preferred_element_type=F32)

    hidden = (gate[...] * jax.nn.sigmoid(gate[...]) * up[...]).astype(BF)

    @pl.loop(0, 2 * NX)
    def _(i):
        cols = column(off_out, i, width)
        rows[i] = jnp.dot(hidden, w2[:, cols], preferred_element_type=F32).astype(BF)

    store_rows(out_pieces, rows)


def backward_kernel(width, off_in, off_out, *refs):
    pieces, (wg, wu, w2, gate_ref, up_ref), outs = (
        refs[:NP],
        refs[NP : NP + 5],
        refs[NP + 5 :],
    )
    out_pieces, (rows, hid_ref) = outs[:NP], outs[NP:]
    load_rows(pieces, rows)
    hid_ref[...] = jnp.zeros_like(hid_ref)

    @pl.loop(0, 2 * NX)
    def _(i):
        cols = column(off_in, i, width)
        hid_ref[...] += lax.dot_general(
            rows[i], w2[:, cols], NT, preferred_element_type=F32
        )

    hid, gate = hid_ref[...], gate_ref[...]
    sigma = jax.nn.sigmoid(gate)
    gate_grad = (hid * up_ref[...] * sigma * (1.0 + gate * (1.0 - sigma))).astype(BF)
    up_grad = (hid * gate * sigma).astype(BF)

    @pl.loop(0, 2 * NX)
    def _(i):
        cols = column(off_out, i, width)
        o = jnp.dot(gate_grad, wg[:, cols], preferred_element_type=F32)
        o = o + jnp.dot(up_grad, wu[:, cols], preferred_element_type=F32)
        rows[i] = o.astype(BF)

    store_rows(out_pieces, rows)


def call(body, name, arrays, off_in, off_out, rows, width, hidden, extra, scratch):
    piece = jax.ShapeDtypeStruct((NY, rows // 2 // NY, width), BF)
    out = [piece] * NP + extra
    return pl.pallas_call(
        functools.partial(body, width),
        name=name,
        out_shape=out,
        in_specs=[pl.BlockSpec(memory_space=pltpu.SMEM)] * 2
        + [pl.BlockSpec(memory_space=pltpu.VMEM)] * len(arrays),
        out_specs=[pl.BlockSpec(memory_space=pltpu.VMEM)] * len(out),
        scratch_shapes=[pltpu.VMEM((2 * NX, rows, width), BF)] + scratch,
        compiler_params=pltpu.CompilerParams(vmem_limit_bytes=VMEM_LIMIT),
        cost_estimate=pl.CostEstimate(
            flops=6 * rows * width * 8 * hidden,
            bytes_accessed=14 << 20,
            transcendentals=rows * hidden,
        ),
    )(off_in, off_out, *arrays)


def on_device(tokens, out_grad, gate_values, routing, gate_weight, up_weight, down_weight):
    width = tokens.shape[1]
    cut = lax.axis_index("cuts")
    x, c = cut // 2, cut % 2
    wg = jnp.swapaxes(gate_weight[0], 0, 1)
    wu = jnp.swapaxes(up_weight[0], 0, 1)
    w2 = down_weight[0]
    hidden = w2.shape[0]
    k = jnp.arange(NX, dtype=jnp.int32)
    dc = jnp.arange(2, dtype=jnp.int32)[:, None]
    core = (c + dc) % 2
    off_in = ((x - k + NX) % NX * 2 + core).reshape(-1)
    off_out = ((x + k) % NX * 2 + core).reshape(-1)
    rows = NY * E * CAP

    select, weight = slots_of(routing, gate_values)
    pick = select.astype(BF).T
    send_x = jnp.dot(pick, tokens, preferred_element_type=F32).astype(BF)
    slot_gate = jnp.sum(weight, axis=0)
    send_dy = jnp.dot(pick, out_grad, preferred_element_type=F32)
    send_dy = (slot_gate[:, None] * send_dy).astype(BF)
    send = jnp.concatenate(
        [send_x.reshape(E, CAP, width), send_dy.reshape(E, CAP, width)], axis=1
    )
    got = swap_z(send).reshape(2, E // 2, 2, CAP, width)
    got = jnp.swapaxes(got, 1, 2).reshape(2, 2, -1, width)

    fa, fb = first_gather(got[0], got[1])

    def gather(i):
        pa, pb = second_gather(
            jnp.stack([v[i] for v in fa]), jnp.stack([v[i] for v in fb])
        )
        own = [*pa, *pb]
        return own + [to_core(v) for v in own]

    xs, dys = gather(0), gather(1)
    pre = [jax.ShapeDtypeStruct((rows, hidden), F32)] * 2
    res = call(
        forward_kernel, "forward", [*xs, wg, wu, w2],
        off_in, off_out, rows, width, hidden, pre, [],
    )
    outs, gate, up = res[:NP], res[NP], res[NP + 1]
    ins = call(
        backward_kernel, "backward", [*dys, wg, wu, w2, gate, up],
        off_in, off_out, rows, width, hidden, [],
        [pltpu.VMEM((rows, hidden), F32)],
    )

    def scatter(p):
        s = [add(p[i], to_core(p[i + NX + NY])) for i in range(NX + NY)]
        return first_scatter(s[:NX], s[NX:])

    ya, yb = scatter(outs)
    ga, gb = scatter(ins)
    ta = jnp.stack([ya, ga], axis=1)
    tb = jnp.stack([yb, gb], axis=1)
    ra, rb = second_scatter([ta[d] for d in range(4)], [tb[d] for d in range(4)])
    back = jnp.stack([ra, rb]).reshape(2, 2, E // 2, CAP, width)
    back = jnp.swapaxes(back, 1, 2).reshape(E, 2 * CAP, width)
    back = swap_z(back)
    back_y = back[:, :CAP].reshape(E * CAP, width)
    back_dx = back[:, CAP:].reshape(E * CAP, width)
    mixed = jnp.dot(weight, back_y.astype(F32), precision=lax.Precision.HIGHEST)
    grad = jnp.dot(select.astype(BF), back_dx, preferred_element_type=F32)
    return mixed.astype(BF), grad.astype(BF)


def solution(mesh):
    return jax.shard_map(
        on_device,
        mesh=mesh,
        in_specs=(
            P("dp", "cuts"),
            P("dp", "cuts"),
            P("dp", None),
            P("dp", None),
            P("dp", None, "cuts"),
            P("dp", None, "cuts"),
            P("dp", "cuts", None),
        ),
        out_specs=(P("dp", "cuts"), P("dp", "cuts")),
        check_vma=False,
    )
```

```python
import jax
import jax.numpy as jnp
from jax import lax
from jax.experimental import pallas as pl
from jax.experimental.pallas import tpu as pltpu
from jax.sharding import PartitionSpec as P

E = 8
NY = 4
NX = 4
CAP = 8
BF = jnp.bfloat16
F32 = jnp.float32
NT = (((1,), (1,)), ((), ()))
VMEM_LIMIT = 20 << 20


def swap_z(v):
    groups = [[z * NY + y for z in range(E)] for y in range(NY)]
    return lax.all_to_all(v, "dp", 0, 0, axis_index_groups=groups, tiled=True)


def to_y(v, d):
    perm = [(z * NY + y, z * NY + (y + d) % NY) for z in range(E) for y in range(NY)]
    return lax.ppermute(v, "dp", perm)


def to_x(v, d):
    perm = [(x * 2 + c, (x + d) % NX * 2 + c) for x in range(NX) for c in range(2)]
    return lax.ppermute(v, "cuts", perm)


def to_core(v):
    return lax.ppermute(v, "cuts", [(i, i ^ 1) for i in range(2 * NX)])


def slots_of(routing, gate_values):
    hit = routing[:, :, None] == jnp.arange(E, dtype=jnp.int32)
    chosen = jnp.any(hit, axis=1)
    gates = jnp.sum(jnp.where(hit, gate_values[:, :, None], 0.0), axis=1)
    rows = routing.shape[0]
    below = jnp.arange(rows)[:, None] > jnp.arange(rows)[None, :]
    position = jnp.sum(
        jnp.where(below[:, :, None] & chosen[None, :, :], 1, 0), axis=1
    )
    slot = position[:, :, None] == jnp.arange(CAP, dtype=jnp.int32)
    select = chosen[:, :, None] & slot
    weight = jnp.where(select, gates[:, :, None], 0.0)
    return select.reshape(rows, E * CAP), weight.reshape(rows, E * CAP)


def first_gather(a, b):
    order = (1, 3, 2)
    ra, rb = {0: a}, {0: b}
    for d in order:
        ra[d] = to_y(a, d)
        rb[d] = to_x(b, d)
    return [ra[d] for d in range(4)], [rb[d] for d in range(4)]


def second_gather(a, b):
    a, b = lax.optimization_barrier((a, b))
    ra, rb = {0: a}, {0: b}
    for d in (2, 1, 3):
        ra[d] = to_x(a, d)
        rb[d] = to_y(b, d)
    own = [ra[d] for d in range(4)] + [rb[d] for d in range(4)]
    return own, [to_core(v) for v in own]


def add(*parts):
    total = parts[0].astype(F32)
    for p in parts[1:]:
        total = total + p.astype(F32)
    return total.astype(BF)


def first_scatter(sa, sb):
    sa, sb = lax.optimization_barrier((sa, sb))
    ra, rb = [sa[0]], [sb[0]]
    for d in (2, 1, 3):
        ra.append(to_x(sa[d], d))
        rb.append(to_y(sb[d], -d))
    return add(*ra), add(*rb)


def second_scatter(ta, tb):
    ta, tb = lax.optimization_barrier((ta, tb))
    ra, rb = [ta[0]], [tb[0]]
    for d in (2, 1, 3):
        ra.append(to_y(ta[d], -d))
        rb.append(to_x(tb[d], d))
    return add(*ra), add(*rb)


def weight_copies(cols, width, weights, buf, sem):
    copies = []
    for k in range(NX):
        at = pl.ds(pl.multiple_of(cols[k] * width, 128), width)
        copies.append(
            [
                pltpu.make_async_copy(w.at[:, at], buf.at[i, k], sem.at[i, k])
                for i, w in enumerate(weights)
            ]
        )
    return copies


def fetch_weights(cols, weights, buf, sem):
    width = buf.shape[-1]
    for block in weight_copies(cols, width, weights, buf, sem):
        for copy in block:
            copy.start()

    def wait(k):
        for i, w in enumerate(weights):
            at = pl.ds(0, width)
            pltpu.make_async_copy(w.at[:, at], buf.at[i, k], sem.at[i, k]).wait()

    return wait


def load_rows(pieces, rows):
    half = rows.shape[2] // 2
    step = half // NY
    for i in range(2):
        for k in range(NX):
            rows[k, i, :half] = pieces[k][i].reshape(half, -1)
            for j in range(NY):
                at = half + j * step
                rows[k, i, at : at + step] = pieces[NX + j][i, k]


def contract(wait, rows, buf, gate, up, hid):
    @pl.loop(0, NX)
    def _(k):
        wait(k)
        r = rows[k, 0]
        gate[...] += lax.dot_general(r, buf[0, k], NT, preferred_element_type=F32)
        up[...] += lax.dot_general(r, buf[1, k], NT, preferred_element_type=F32)
        hid[...] += lax.dot_general(
            rows[k, 1], buf[2, k], NT, preferred_element_type=F32
        )


def expand(wait, hidden, gate_grad, up_grad, buf, out_a, out_b):
    half = hidden.shape[0] // 2
    step = half // NY

    def put(k, i, value):
        out_a[k, i] = value[:half].reshape(NY, step, -1)
        for j in range(NY):
            out_b[j, i, k] = value[half + j * step : half + (j + 1) * step]

    @pl.loop(0, NX)
    def _(k):
        at = (NX - k) & (NX - 1)
        if wait is not None:
            wait(at)
        o = jnp.dot(hidden[...], buf[2, at], preferred_element_type=F32)
        put(k, 0, o.astype(BF))
        o = jnp.dot(gate_grad[...], buf[0, at], preferred_element_type=F32)
        o = o + jnp.dot(up_grad[...], buf[1, at], preferred_element_type=F32)
        put(k, 1, o.astype(BF))


def own_kernel(cols, *refs):
    pieces, weights, (gate, up, hid, rows, buf, sem) = refs[:8], refs[8:11], refs[11:]
    wait = fetch_weights(cols, weights, buf, sem)
    load_rows(pieces, rows)
    for ref in (gate, up, hid):
        ref[...] = jnp.zeros_like(ref)
    contract(wait, rows, buf, gate, up, hid)


def other_kernel(cols, *refs):
    pieces, weights, partial, rest = refs[:8], refs[8:11], refs[11:14], refs[14:]
    out_a, out_b, hidden, gate_grad, up_grad, rows, gate, up, hid, buf, sem = rest
    wait = fetch_weights(cols, weights, buf, sem)
    load_rows(pieces, rows)
    for ref, part in zip((gate, up, hid), partial):
        ref[...] = part[...]
    contract(wait, rows, buf, gate, up, hid)
    g, h = gate[...], hid[...]
    sigma = jax.nn.sigmoid(g)
    hidden[...] = (g * sigma * up[...]).astype(BF)
    gate_grad[...] = (h * up[...] * sigma * (1.0 + g * (1.0 - sigma))).astype(BF)
    up_grad[...] = (h * g * sigma).astype(BF)
    expand(None, hidden, gate_grad, up_grad, buf, out_a, out_b)


def last_kernel(cols, *refs):
    (hidden, gate_grad, up_grad), weights, (out_a, out_b, buf, sem) = (
        refs[:3],
        refs[3:6],
        refs[6:],
    )
    wait = fetch_weights(cols, weights, buf, sem)
    expand(wait, hidden, gate_grad, up_grad, buf, out_a, out_b)


def call(body, name, cols, arrays, weights, partial, out, scratch, products):
    hidden, width = weights[0].shape[0], weights[0].shape[1] // (2 * NX)
    rows = E * CAP * NY
    return pl.pallas_call(
        body,
        name=name,
        out_shape=out,
        in_specs=[pl.BlockSpec(memory_space=pltpu.SMEM)]
        + [pl.BlockSpec(memory_space=pltpu.VMEM)] * len(arrays)
        + [pl.BlockSpec(memory_space=pl.ANY)] * 3
        + [pl.BlockSpec(memory_space=pltpu.VMEM)] * len(partial),
        out_specs=[pl.BlockSpec(memory_space=pltpu.VMEM)] * len(out),
        scratch_shapes=scratch
        + [
            pltpu.VMEM((3, NX, hidden, width), BF),
            pltpu.SemaphoreType.DMA((3, NX)),
        ],
        compiler_params=pltpu.CompilerParams(vmem_limit_bytes=VMEM_LIMIT),
        cost_estimate=pl.CostEstimate(
            flops=2 * products * rows * width * NX * hidden,
            bytes_accessed=7 << 20,
            transcendentals=0,
        ),
    )(cols, *arrays, *weights, *partial)


def on_device(tokens, out_grad, gate_values, routing, gate_weight, up_weight, down_weight):
    width = tokens.shape[1]
    cut = lax.axis_index("cuts")
    x, c = cut // 2, cut % 2
    wg = jnp.swapaxes(gate_weight[0], 0, 1)
    wu = jnp.swapaxes(up_weight[0], 0, 1)
    w2 = down_weight[0]
    hidden = w2.shape[0]
    k = jnp.arange(NX, dtype=jnp.int32)
    own_cols = (x - k + NX) % NX * 2 + c
    other_cols = (x - k + NX) % NX * 2 + (1 - c)
    rows = NY * E * CAP

    select, weight = slots_of(routing, gate_values)
    pick = select.astype(BF).T
    send_x = jnp.dot(pick, tokens, preferred_element_type=F32).astype(BF)
    slot_gate = jnp.sum(weight, axis=0)
    send_dy = jnp.dot(pick, out_grad, preferred_element_type=F32)
    send_dy = (slot_gate[:, None] * send_dy).astype(BF)
    send = jnp.concatenate(
        [send_x.reshape(E, CAP, width), send_dy.reshape(E, CAP, width)], axis=1
    )
    got = swap_z(send).reshape(2, E // 2, 2, CAP, width)
    got = jnp.swapaxes(got, 1, 2).reshape(2, 2, -1, width)

    fa, fb = first_gather(got[0], got[1])

    own, other = second_gather(jnp.stack(fa, axis=1), jnp.stack(fb, axis=1))

    weights = (wg, wu, w2)
    pre = [jax.ShapeDtypeStruct((rows, hidden), F32)] * 3
    act = [jax.ShapeDtypeStruct((rows, hidden), BF)] * 3
    pieces = [jax.ShapeDtypeStruct((4, 2, 4, rows // 8, width), BF)] * 2
    row_buf = [pltpu.VMEM((NX, 2, rows, width), BF)]
    pre_buf = [pltpu.VMEM((rows, hidden), F32)] * 3
    partial = call(own_kernel, "own", own_cols, own, weights, [], pre, row_buf, 3)
    far_a, far_b, *act = call(
        other_kernel, "other", other_cols, other, weights, partial,
        pieces + act, row_buf + pre_buf, 6,
    )
    near_a, near_b = call(
        last_kernel, "last", own_cols, act, weights, [], pieces, [], 3
    )
    got_a, got_b = to_core(far_a), to_core(far_b)
    sa = [add(near_a[d], got_a[d]) for d in range(4)]
    sb = [add(near_b[d], got_b[d]) for d in range(4)]
    ta, tb = first_scatter(sa, sb)
    ra, rb = second_scatter(
        [ta[:, d] for d in range(4)], [tb[:, d] for d in range(4)]
    )
    back = jnp.stack([ra, rb]).reshape(2, 2, E // 2, CAP, width)
    back = jnp.swapaxes(back, 1, 2).reshape(E, 2 * CAP, width)
    back = swap_z(back)
    back_y = back[:, :CAP].reshape(E * CAP, width)
    back_dx = back[:, CAP:].reshape(E * CAP, width)
    mixed = jnp.dot(weight, back_y.astype(F32), precision=lax.Precision.HIGHEST)
    grad = jnp.dot(select.astype(BF), back_dx, preferred_element_type=F32)
    return mixed.astype(BF), grad.astype(BF)


def solution(mesh):
    return jax.shard_map(
        on_device,
        mesh=mesh,
        in_specs=(
            P("dp", "cuts"),
            P("dp", "cuts"),
            P("dp", None),
            P("dp", None),
            P("dp", None, "cuts"),
            P("dp", None, "cuts"),
            P("dp", "cuts", None),
        ),
        out_specs=(P("dp", "cuts"), P("dp", "cuts")),
        check_vma=False,
    )
```

```python
import jax
import jax.numpy as jnp
from jax import lax
from jax.experimental import pallas as pl
from jax.experimental.pallas import tpu as pltpu
from jax.sharding import PartitionSpec as P

E = 8
NY = 4
NX = 4
CAP = 8
BF = jnp.bfloat16
F32 = jnp.float32
NT = (((1,), (1,)), ((), ()))
VMEM_LIMIT = {"own": 20, "other": 24, "last": 16}


def swap_z(v):
    groups = [[z * NY + y for z in range(E)] for y in range(NY)]
    return lax.all_to_all(v, "dp", 0, 0, axis_index_groups=groups, tiled=True)


def partner(i, q):
    if q == 1:
        return i ^ 1
    return (i + (1 if i % 2 else 3)) % 4 if q == 2 else i ^ 2


def to_y(v, q):
    perm = [(z * NY + y, z * NY + partner(y, q)) for z in range(E) for y in range(NY)]
    return lax.ppermute(v, "dp", perm)


def to_x(v, q):
    perm = [(x * 2 + c, partner(x, q) * 2 + c) for x in range(NX) for c in range(2)]
    return lax.ppermute(v, "cuts", perm)


def to_core(v):
    return lax.ppermute(v, "cuts", [(i, i ^ 1) for i in range(2 * NX)])


def slots_of(routing, gate_values):
    hit = routing[:, :, None] == jnp.arange(E, dtype=jnp.int32)
    chosen = jnp.any(hit, axis=1)
    gates = jnp.sum(jnp.where(hit, gate_values[:, :, None], 0.0), axis=1)
    rows = routing.shape[0]
    below = jnp.arange(rows)[:, None] > jnp.arange(rows)[None, :]
    position = jnp.sum(
        jnp.where(below[:, :, None] & chosen[None, :, :], 1, 0), axis=1
    )
    slot = position[:, :, None] == jnp.arange(CAP, dtype=jnp.int32)
    select = chosen[:, :, None] & slot
    weight = jnp.where(select, gates[:, :, None], 0.0)
    return select.reshape(rows, E * CAP), weight.reshape(rows, E * CAP)


def first_gather(a, b):
    a, b = a[:, None], b[:, None]
    for q in (1, 2):
        ga, gb = lax.optimization_barrier((to_y(a, q), to_x(b, q)))
        a = jnp.concatenate([a, ga], axis=1)
        b = jnp.concatenate([b, gb], axis=1)
    return a, b


def second_gather(a, b):
    a, b = lax.optimization_barrier((a, b))
    got = {}
    for q in (3, 1, 2):
        got[q] = to_x(a, q), to_y(b, q)
    got = lax.optimization_barrier(got)
    own = [a] + [got[q][0] for q in (1, 2, 3)] + [b] + [got[q][1] for q in (1, 2, 3)]
    own = list(lax.optimization_barrier(tuple(own)))
    return own, [to_core(v) for v in own]


def add(*parts):
    total = parts[0].astype(F32)
    for p in parts[1:]:
        total = total + p.astype(F32)
    return total.astype(BF)


def first_scatter(sa, sb):
    sa, sb = lax.optimization_barrier((sa, sb))
    got = {}
    for q in (3, 1, 2):
        got[q] = to_x(sa[q], q), to_y(sb[q], q)
    got = lax.optimization_barrier(got)
    ra = add(sa[0], *[got[q][0] for q in (1, 2, 3)])
    rb = add(sb[0], *[got[q][1] for q in (1, 2, 3)])
    return ra, rb


def second_scatter(a, b):
    for q in (2, 1):
        keep = a.shape[1] // 2
        a, b = lax.optimization_barrier((a, b))
        got = to_y(a[:, keep:], q), to_x(b[:, keep:], q)
        ga, gb = lax.optimization_barrier(got)
        a, b = add(a[:, :keep], ga), add(b[:, :keep], gb)
    return a[:, 0], b[:, 0]


def fetch_weights(cols, weights, buf, sem):
    hidden, width = weights[0].shape[0], buf.shape[-1]

    def copy(i, k, at):
        rows = pl.ds(i * hidden, hidden)
        return pltpu.make_async_copy(
            weights[i].at[:, pl.ds(at, width)], buf.at[k, rows], sem.at[k, i]
        )

    for k in range(NX):
        for i in range(3):
            copy(i, k, pl.multiple_of(cols[k] * width, 128)).start()

    def wait(k):
        for i in range(3):
            copy(i, k, 0).wait()

    return wait


def load_rows(pieces, rows):
    half = rows.shape[2] // 2
    step = half // NY
    for i in range(2):
        for k in range(NX):
            rows[k, i, :half] = pieces[k][i].reshape(half, -1)
            for j in range(NY):
                at = half + j * step
                rows[k, i, at : at + step] = pieces[NX + j][i, k]


def contract(wait, rows, buf, acc):
    two = acc.shape[0] // 3 * 2

    @pl.loop(0, NX)
    def _(k):
        wait(k)
        acc[:two] += lax.dot_general(
            buf[k, :two], rows[k, 0], NT, preferred_element_type=F32
        )
        acc[two:] += lax.dot_general(
            buf[k, two:], rows[k, 1], NT, preferred_element_type=F32
        )


def expand(wait, hidden, grads, buf, out_a, out_b):
    half = hidden.shape[0] // 2
    step = half // NY
    two = grads.shape[1]

    def put(k, i, value):
        out_a[k, i] = value[:half].reshape(NY, step, -1)
        for j in range(NY):
            out_b[j, i, k] = value[half + j * step : half + (j + 1) * step]

    @pl.loop(0, NX)
    def _(k):
        if wait is not None:
            wait(k)
        o = jnp.dot(hidden[...], buf[k, two:], preferred_element_type=F32)
        put(k, 0, o.astype(BF))
        o = jnp.dot(grads[...], buf[k, :two], preferred_element_type=F32)
        put(k, 1, o.astype(BF))


def own_kernel(cols, *refs):
    pieces, weights, (acc, rows, buf, sem) = refs[:8], refs[8:11], refs[11:]
    wait = fetch_weights(cols, weights, buf, sem)
    load_rows(pieces, rows)
    acc[...] = jnp.zeros_like(acc)
    contract(wait, rows, buf, acc)


def other_kernel(cols, *refs):
    pieces, weights, partial, rest = refs[:8], refs[8:11], refs[11], refs[12:]
    out_a, out_b, hidden, grads, rows, acc, buf, sem = rest
    wait = fetch_weights(cols, weights, buf, sem)
    load_rows(pieces, rows)
    acc[...] = partial[...]
    contract(wait, rows, buf, acc)
    one = acc.shape[0] // 3
    g, u, h = acc[:one], acc[one : 2 * one], acc[2 * one :]
    sigma = jax.nn.sigmoid(g)
    hidden[...] = (g * sigma * u).T.astype(BF)
    gate_grad = h * u * sigma * (1.0 + g * (1.0 - sigma))
    grads[...] = jnp.concatenate([gate_grad, h * g * sigma], axis=0).T.astype(BF)
    expand(None, hidden, grads, buf, out_a, out_b)


def last_kernel(cols, *refs):
    (hidden, grads), weights, (out_a, out_b, buf, sem) = refs[:2], refs[2:5], refs[5:]
    wait = fetch_weights(cols, weights, buf, sem)
    expand(wait, hidden, grads, buf, out_a, out_b)


def call(body, name, cols, arrays, weights, partial, out, scratch, products):
    hidden, width = weights[0].shape[0], weights[0].shape[1] // (2 * NX)
    rows = E * CAP * NY
    return pl.pallas_call(
        body,
        name=name,
        out_shape=out,
        in_specs=[pl.BlockSpec(memory_space=pltpu.SMEM)]
        + [pl.BlockSpec(memory_space=pltpu.VMEM)] * len(arrays)
        + [pl.BlockSpec(memory_space=pltpu.HBM)] * 3
        + [pl.BlockSpec(memory_space=pltpu.VMEM)] * len(partial),
        out_specs=[pl.BlockSpec(memory_space=pltpu.VMEM)] * len(out),
        scratch_shapes=scratch
        + [
            pltpu.VMEM((NX, 3 * hidden, width), BF),
            pltpu.SemaphoreType.DMA((NX, 3)),
        ],
        compiler_params=pltpu.CompilerParams(vmem_limit_bytes=VMEM_LIMIT[name] << 20),
        cost_estimate=pl.CostEstimate(
            flops=2 * products * rows * width * NX * hidden,
            bytes_accessed=7 << 20,
            transcendentals=0,
        ),
    )(cols, *arrays, *weights, *partial)


def on_device(tokens, out_grad, gate_values, routing, gate_weight, up_weight, down_weight):
    width = tokens.shape[1]
    cut = lax.axis_index("cuts")
    x, c = cut // 2, cut % 2
    wg = jnp.swapaxes(gate_weight[0], 0, 1)
    wu = jnp.swapaxes(up_weight[0], 0, 1)
    w2 = down_weight[0]
    hidden = w2.shape[0]
    own_cols = jnp.stack([x, x ^ 1, (x + 3 + 2 * (x % 2)) % NX, x ^ 2]) * 2 + c
    other_cols = own_cols ^ 1
    rows = NY * E * CAP

    select, weight = slots_of(routing, gate_values)
    pick = select.astype(BF).T
    send_x = jnp.dot(pick, tokens, preferred_element_type=F32).astype(BF)
    slot_gate = jnp.sum(weight, axis=0)
    send_dy = jnp.dot(pick, out_grad, preferred_element_type=F32)
    send_dy = (slot_gate[:, None] * send_dy).astype(BF)
    send = jnp.concatenate(
        [send_x.reshape(E, CAP, width), send_dy.reshape(E, CAP, width)], axis=1
    )
    got = swap_z(send).reshape(2, E // 2, 2, CAP, width)
    got = jnp.swapaxes(got, 1, 2).reshape(2, 2, -1, width)

    own, other = second_gather(*first_gather(got[0], got[1]))

    weights = [pltpu.with_memory_space_constraint(w, pltpu.HBM) for w in (wg, wu, w2)]
    pre = jax.ShapeDtypeStruct((3 * hidden, rows), F32)
    act = [
        jax.ShapeDtypeStruct((rows, hidden), BF),
        jax.ShapeDtypeStruct((rows, 2 * hidden), BF),
    ]
    pieces = [jax.ShapeDtypeStruct((4, 2, 4, rows // 8, width), BF)] * 2
    row_buf = [pltpu.VMEM((NX, 2, rows, width), BF)]
    acc_buf = [pltpu.VMEM(pre.shape, F32)]
    partial = call(own_kernel, "own", own_cols, own, weights, [], [pre], row_buf, 3)
    far_a, far_b, *act = call(
        other_kernel, "other", other_cols, other, weights, partial,
        pieces + act, row_buf + acc_buf, 6,
    )
    near_a, near_b = call(
        last_kernel, "last", own_cols, act, weights, [], pieces, [], 3
    )
    got_a, got_b = to_core(far_a), to_core(far_b)
    sa = [add(near_a[d], got_a[d]) for d in range(4)]
    sb = [add(near_b[d], got_b[d]) for d in range(4)]
    ta, tb = first_scatter(sa, sb)
    ra, rb = second_scatter(ta, tb)
    back = jnp.stack([ra, rb]).reshape(2, 2, E // 2, CAP, width)
    back = jnp.swapaxes(back, 1, 2).reshape(E, 2 * CAP, width)
    back = swap_z(back)
    back_y = back[:, :CAP].reshape(E * CAP, width)
    back_dx = back[:, CAP:].reshape(E * CAP, width)
    mixed = jnp.dot(weight, back_y.astype(F32), precision=lax.Precision.HIGHEST)
    grad = jnp.dot(select.astype(BF), back_dx, preferred_element_type=F32)
    return mixed.astype(BF), grad.astype(BF)


def solution(mesh):
    return jax.shard_map(
        on_device,
        mesh=mesh,
        in_specs=(
            P("dp", "cuts"),
            P("dp", "cuts"),
            P("dp", None),
            P("dp", None),
            P("dp", None, "cuts"),
            P("dp", None, "cuts"),
            P("dp", "cuts", None),
        ),
        out_specs=(P("dp", "cuts"), P("dp", "cuts")),
        check_vma=False,
    )
```

```python
import itertools

import jax
import jax.numpy as jnp
from jax import lax
from jax.experimental import pallas as pl
from jax.experimental.pallas import tpu as pltpu
from jax.sharding import PartitionSpec as P

E = 8
NY = 4
NX = 4
CAP = 8
BF = jnp.bfloat16
F32 = jnp.float32
NT = (((1,), (1,)), ((), ()))
VMEM_LIMIT = {"own": 20, "other": 24, "last": 16}


def swap_z(v):
    groups = [[z * NY + y for z in range(E)] for y in range(NY)]
    return lax.all_to_all(v, "dp", 0, 0, axis_index_groups=groups, tiled=True)


def partner(i, q):
    if q == 1:
        return i ^ 1
    return (i + (1 if i % 2 else 3)) % 4 if q == 2 else i ^ 2


def swap(v, q, along_y):
    def place(z, y, x, c):
        return (z * NY + y) * 2 * NX + x * 2 + c

    perm = []
    for z, y, x, c in itertools.product(range(E), range(NY), range(NX), range(2)):
        if c == along_y:
            to = place(z, partner(y, q), x, c)
        else:
            to = place(z, y, partner(x, q), c)
        perm.append((place(z, y, x, c), to))
    return lax.ppermute(v, ("dp", "cuts"), perm)


def to_core(v):
    return lax.ppermute(v, "cuts", [(i, i ^ 1) for i in range(2 * NX)])


def slots_of(routing, gate_values):
    hit = routing[:, :, None] == jnp.arange(E, dtype=jnp.int32)
    chosen = jnp.any(hit, axis=1)
    gates = jnp.sum(jnp.where(hit, gate_values[:, :, None], 0.0), axis=1)
    rows = routing.shape[0]
    below = jnp.arange(rows)[:, None] > jnp.arange(rows)[None, :]
    position = jnp.sum(
        jnp.where(below[:, :, None] & chosen[None, :, :], 1, 0), axis=1
    )
    slot = position[:, :, None] == jnp.arange(CAP, dtype=jnp.int32)
    select = chosen[:, :, None] & slot
    weight = jnp.where(select, gates[:, :, None], 0.0)
    return select.reshape(rows, E * CAP), weight.reshape(rows, E * CAP)


def gather(v, along_y):
    far, near, next_ = lax.optimization_barrier(
        tuple(swap(v, q, along_y) for q in (3, 1, 2))
    )
    return [v, near, next_, far]


def add(*parts):
    total = parts[0].astype(F32)
    for p in parts[1:]:
        total = total + p.astype(F32)
    return total.astype(BF)


def scatter(parts, along_y):
    parts = lax.optimization_barrier(tuple(parts))
    got = lax.optimization_barrier(
        tuple(swap(parts[q], q, along_y) for q in (3, 1, 2))
    )
    return add(parts[0], *got)


def fetch_weights(info, weights, buf, sem):
    hidden, width = weights[0].shape[0], buf.shape[-1]

    def copy(i, k, at):
        rows = pl.ds(i * hidden, hidden)
        return pltpu.make_async_copy(
            weights[i].at[:, pl.ds(at, width)], buf.at[k, rows], sem.at[k, i]
        )

    for k in range(NX):
        for i in range(3):
            copy(i, k, pl.multiple_of(info[k] * width, 128)).start()

    def wait(k):
        for i in range(3):
            copy(i, k, 0).wait()

    return wait


def order(info, b, a):
    first = info[NX] == 0
    return jnp.where(first, b, a), jnp.where(first, a, b)


def load_rows(info, pieces, rows):
    step = rows.shape[2] // NY
    for b in range(4):
        for a in range(4):
            k, j = order(info, b, a)
            at = pl.ds(pl.multiple_of(j * step, step), step)
            for i in range(2):
                rows[k, i, at] = pieces[b][a, i]


def contract(wait, rows, buf, acc):
    two = acc.shape[0] // 3 * 2

    @pl.loop(0, NX)
    def _(k):
        wait(k)
        acc[:two] += lax.dot_general(
            buf[k, :two], rows[k, 0], NT, preferred_element_type=F32
        )
        acc[two:] += lax.dot_general(
            buf[k, two:], rows[k, 1], NT, preferred_element_type=F32
        )


def expand(info, wait, hidden, grads, buf, out):
    step = hidden.shape[0] // NY
    two = grads.shape[1]

    def put(k, i, value):
        for j in range(NY):
            b, a = order(info, k, j)
            out[b, a, i] = value[j * step : (j + 1) * step]

    @pl.loop(0, NX)
    def _(k):
        if wait is not None:
            wait(k)
        o = jnp.dot(hidden[...], buf[k, two:], preferred_element_type=F32)
        put(k, 0, o.astype(BF))
        o = jnp.dot(grads[...], buf[k, :two], preferred_element_type=F32)
        put(k, 1, o.astype(BF))


def own_kernel(info, *refs):
    pieces, weights, (acc, rows, buf, sem) = refs[:4], refs[4:7], refs[7:]
    wait = fetch_weights(info, weights, buf, sem)
    load_rows(info, pieces, rows)
    acc[...] = jnp.zeros_like(acc)
    contract(wait, rows, buf, acc)


def other_kernel(info, *refs):
    pieces, weights, partial, rest = refs[:4], refs[4:7], refs[7], refs[8:]
    out, hidden, grads, rows, acc, buf, sem = rest
    wait = fetch_weights(info, weights, buf, sem)
    load_rows(info, pieces, rows)
    acc[...] = partial[...]
    contract(wait, rows, buf, acc)
    one = acc.shape[0] // 3
    g, u, h = acc[:one], acc[one : 2 * one], acc[2 * one :]
    sigma = jax.nn.sigmoid(g)
    hidden[...] = (g * sigma * u).T.astype(BF)
    gate_grad = h * u * sigma * (1.0 + g * (1.0 - sigma))
    grads[...] = jnp.concatenate([gate_grad, h * g * sigma], axis=0).T.astype(BF)
    expand(info, None, hidden, grads, buf, out)


def last_kernel(info, *refs):
    (hidden, grads), weights, (out, buf, sem) = refs[:2], refs[2:5], refs[5:]
    wait = fetch_weights(info, weights, buf, sem)
    expand(info, wait, hidden, grads, buf, out)


def call(body, name, info, arrays, weights, partial, out, scratch, products):
    hidden, width = weights[0].shape[0], weights[0].shape[1] // (2 * NX)
    rows = E * CAP * NY
    return pl.pallas_call(
        body,
        name=name,
        out_shape=out,
        in_specs=[pl.BlockSpec(memory_space=pltpu.SMEM)]
        + [pl.BlockSpec(memory_space=pltpu.VMEM)] * len(arrays)
        + [pl.BlockSpec(memory_space=pltpu.HBM)] * 3
        + [pl.BlockSpec(memory_space=pltpu.VMEM)] * len(partial),
        out_specs=[pl.BlockSpec(memory_space=pltpu.VMEM)] * len(out),
        scratch_shapes=scratch
        + [
            pltpu.VMEM((NX, 3 * hidden, width), BF),
            pltpu.SemaphoreType.DMA((NX, 3)),
        ],
        compiler_params=pltpu.CompilerParams(vmem_limit_bytes=VMEM_LIMIT[name] << 20),
        cost_estimate=pl.CostEstimate(
            flops=2 * products * rows * width * NX * hidden,
            bytes_accessed=7 << 20,
            transcendentals=0,
        ),
    )(info, *arrays, *weights, *partial)


def on_device(tokens, out_grad, gate_values, routing, gate_weight, up_weight, down_weight):
    width = tokens.shape[1]
    cut = lax.axis_index("cuts")
    x, c = cut // 2, cut % 2
    wg = jnp.swapaxes(gate_weight[0], 0, 1)
    wu = jnp.swapaxes(up_weight[0], 0, 1)
    w2 = down_weight[0]
    hidden = w2.shape[0]
    steps = jnp.arange(NX + 1)
    there = jnp.where(steps == 2, (x + 3 + 2 * (x % 2)) % NX, x ^ steps)
    there = jnp.where(steps == 3, x ^ 2, there)
    own_info = jnp.where(steps < NX, there * 2 + c, c)
    other_info = own_info ^ 1
    rows = NY * E * CAP

    select, weight = slots_of(routing, gate_values)
    pick = select.astype(BF).T
    send_x = jnp.dot(pick, tokens, preferred_element_type=F32).astype(BF)
    slot_gate = jnp.sum(weight, axis=0)
    send_dy = jnp.dot(pick, out_grad, preferred_element_type=F32)
    send_dy = (slot_gate[:, None] * send_dy).astype(BF)
    send = jnp.concatenate(
        [send_x.reshape(E, CAP, width), send_dy.reshape(E, CAP, width)], axis=1
    )
    got = swap_z(send).reshape(E, 2, CAP, width)
    got = jnp.swapaxes(got, 0, 1).reshape(2, E * CAP, width)

    own = gather(jnp.stack(gather(got, 0)), 1)
    own = list(lax.optimization_barrier(tuple(own)))
    other = [to_core(v) for v in own]

    weights = [pltpu.with_memory_space_constraint(w, pltpu.HBM) for w in (wg, wu, w2)]
    pre = jax.ShapeDtypeStruct((3 * hidden, rows), F32)
    act = [
        jax.ShapeDtypeStruct((rows, hidden), BF),
        jax.ShapeDtypeStruct((rows, 2 * hidden), BF),
    ]
    pieces = [jax.ShapeDtypeStruct((4, 4, 2, rows // 4, width), BF)]
    row_buf = [pltpu.VMEM((NX, 2, rows, width), BF)]
    acc_buf = [pltpu.VMEM(pre.shape, F32)]
    partial = call(own_kernel, "own", own_info, own, weights, [], [pre], row_buf, 3)
    far, *act = call(
        other_kernel, "other", other_info, other, weights, partial,
        pieces + act, row_buf + acc_buf, 6,
    )
    (near,) = call(last_kernel, "last", own_info, act, weights, [], pieces, [], 3)
    got = to_core(far)
    sums = scatter([add(near[b], got[b]) for b in range(4)], 1)
    back = scatter([sums[a] for a in range(4)], 0)
    back = back.reshape(2, E, CAP, width)
    back = jnp.swapaxes(back, 0, 1).reshape(E, 2 * CAP, width)
    back = swap_z(back)
    back_y = back[:, :CAP].reshape(E * CAP, width)
    back_dx = back[:, CAP:].reshape(E * CAP, width)
    mixed = jnp.dot(weight, back_y.astype(F32), precision=lax.Precision.HIGHEST)
    grad = jnp.dot(select.astype(BF), back_dx, preferred_element_type=F32)
    return mixed.astype(BF), grad.astype(BF)


def solution(mesh):
    return jax.shard_map(
        on_device,
        mesh=mesh,
        in_specs=(
            P("dp", "cuts"),
            P("dp", "cuts"),
            P("dp", None),
            P("dp", None),
            P("dp", None, "cuts"),
            P("dp", None, "cuts"),
            P("dp", "cuts", None),
        ),
        out_specs=(P("dp", "cuts"), P("dp", "cuts")),
        check_vma=False,
    )
```

```python
import itertools

import jax
import jax.numpy as jnp
from jax import lax
from jax.experimental import pallas as pl
from jax.experimental.pallas import tpu as pltpu
from jax.sharding import PartitionSpec as P

E = 8
NY = 4
NX = 4
CAP = 8
BF = jnp.bfloat16
F32 = jnp.float32
NT = (((1,), (1,)), ((), ()))
VMEM_LIMIT = {"own": 8, "other": 12, "last": 4}


def swap_z(v):
    groups = [[z * NY + y for z in range(E)] for y in range(NY)]
    return lax.all_to_all(v, "dp", 0, 0, axis_index_groups=groups, tiled=True)


def partner(i, q):
    if q == 1:
        return i ^ 1
    return (i + (1 if i % 2 else 3)) % 4 if q == 2 else i ^ 2


def swap(v, q, along_y):
    def place(z, y, x, c):
        return (z * NY + y) * 2 * NX + x * 2 + c

    perm = []
    for z, y, x, c in itertools.product(range(E), range(NY), range(NX), range(2)):
        if c == along_y:
            to = place(z, partner(y, q), x, c)
        else:
            to = place(z, y, partner(x, q), c)
        perm.append((place(z, y, x, c), to))
    return lax.ppermute(v, ("dp", "cuts"), perm)


def to_core(v):
    return lax.ppermute(v, "cuts", [(i, i ^ 1) for i in range(2 * NX)])


def slots_of(routing, gate_values):
    hit = routing[:, :, None] == jnp.arange(E, dtype=jnp.int32)
    chosen = jnp.any(hit, axis=1)
    gates = jnp.sum(jnp.where(hit, gate_values[:, :, None], 0.0), axis=1)
    rows = routing.shape[0]
    below = jnp.arange(rows)[:, None] > jnp.arange(rows)[None, :]
    position = jnp.sum(
        jnp.where(below[:, :, None] & chosen[None, :, :], 1, 0), axis=1
    )
    slot = position[:, :, None] == jnp.arange(CAP, dtype=jnp.int32)
    select = chosen[:, :, None] & slot
    weight = jnp.where(select, gates[:, :, None], 0.0)
    return select.reshape(rows, E * CAP), weight.reshape(rows, E * CAP)


def gather(v, along_y):
    far, near, next_ = lax.optimization_barrier(
        tuple(swap(v, q, along_y) for q in (3, 1, 2))
    )
    return [v, near, next_, far]


def add(*parts):
    total = parts[0].astype(F32)
    for p in parts[1:]:
        total = total + p.astype(F32)
    return total.astype(BF)


def scatter(parts, along_y):
    parts = lax.optimization_barrier(tuple(parts))
    got = lax.optimization_barrier(
        tuple(swap(parts[q], q, along_y) for q in (3, 1, 2))
    )
    return add(parts[0], *got)


def weights_kernel(infos, *refs):
    weights, bufs, sem = refs[:3], refs[3:5], refs[5]
    hidden, width = weights[0].shape[0], bufs[0].shape[-1]
    copies = []
    for core in range(2):
        for k in range(NX):
            at = pl.ds(pl.multiple_of(infos[core, k] * width, 128), width)
            for i in range(3):
                to = bufs[core].at[k, pl.ds(i * hidden, hidden)]
                copies.append(
                    pltpu.make_async_copy(
                        weights[i].at[:, at], to, sem.at[core, k, i]
                    )
                )
    for copy in copies:
        copy.start()
    for copy in copies:
        copy.wait()


def load_weights(infos, weights, width):
    hidden = weights[0].shape[0]
    return pl.pallas_call(
        weights_kernel,
        name="weights",
        out_shape=[jax.ShapeDtypeStruct((NX, 3 * hidden, width), BF)] * 2,
        in_specs=[pl.BlockSpec(memory_space=pltpu.SMEM)]
        + [pl.BlockSpec(memory_space=pltpu.HBM)] * 3,
        out_specs=[pl.BlockSpec(memory_space=pltpu.VMEM)] * 2,
        scratch_shapes=[pltpu.SemaphoreType.DMA((2, NX, 3))],
        compiler_params=pltpu.CompilerParams(vmem_limit_bytes=4 << 20),
        cost_estimate=pl.CostEstimate(
            flops=0, bytes_accessed=26 << 20, transcendentals=0
        ),
    )(infos, *weights)


def order(info, b, a):
    first = info[NX] == 0
    return jnp.where(first, b, a), jnp.where(first, a, b)


def load_rows(info, pieces, rows):
    step = rows.shape[2] // NY
    for b in range(4):
        for a in range(4):
            k, j = order(info, b, a)
            at = pl.ds(pl.multiple_of(j * step, step), step)
            for i in range(2):
                rows[k, i, at] = pieces[b][a, i]


def contract(rows, buf, acc):
    two = acc.shape[0] // 3 * 2

    @pl.loop(0, NX)
    def _(k):
        acc[:two] += lax.dot_general(
            buf[k, :two], rows[k, 0], NT, preferred_element_type=F32
        )
        acc[two:] += lax.dot_general(
            buf[k, two:], rows[k, 1], NT, preferred_element_type=F32
        )


def expand(info, hidden, grads, buf, out):
    step = hidden.shape[0] // NY
    two = grads.shape[1]

    def put(k, i, value):
        for j in range(NY):
            b, a = order(info, k, j)
            out[b, a, i] = value[j * step : (j + 1) * step]

    @pl.loop(0, NX)
    def _(k):
        o = jnp.dot(hidden[...], buf[k, two:], preferred_element_type=F32)
        put(k, 0, o.astype(BF))
        o = jnp.dot(grads[...], buf[k, :two], preferred_element_type=F32)
        put(k, 1, o.astype(BF))


def own_kernel(info, *refs):
    pieces, (buf, acc, rows) = refs[:4], refs[4:]
    load_rows(info, pieces, rows)
    acc[...] = jnp.zeros_like(acc)
    contract(rows, buf, acc)


def other_kernel(info, *refs):
    pieces, (buf, partial, out, hidden, grads, rows, acc) = refs[:4], refs[4:]
    load_rows(info, pieces, rows)
    acc[...] = partial[...]
    contract(rows, buf, acc)
    one = acc.shape[0] // 3
    g, u, h = acc[:one], acc[one : 2 * one], acc[2 * one :]
    sigma = jax.nn.sigmoid(g)
    hidden[...] = (g * sigma * u).T.astype(BF)
    gate_grad = h * u * sigma * (1.0 + g * (1.0 - sigma))
    grads[...] = jnp.concatenate([gate_grad, h * g * sigma], axis=0).T.astype(BF)
    expand(info, hidden, grads, buf, out)


def last_kernel(info, hidden, grads, buf, out):
    expand(info, hidden, grads, buf, out)


def call(body, name, info, arrays, out, scratch, products, shape):
    rows, hidden, width = shape
    return pl.pallas_call(
        body,
        name=name,
        out_shape=out,
        in_specs=[pl.BlockSpec(memory_space=pltpu.SMEM)]
        + [pl.BlockSpec(memory_space=pltpu.VMEM)] * len(arrays),
        out_specs=[pl.BlockSpec(memory_space=pltpu.VMEM)] * len(out),
        scratch_shapes=scratch,
        compiler_params=pltpu.CompilerParams(vmem_limit_bytes=VMEM_LIMIT[name] << 20),
        cost_estimate=pl.CostEstimate(
            flops=2 * products * rows * width * NX * hidden,
            bytes_accessed=7 << 20,
            transcendentals=0,
        ),
    )(info, *arrays)


def on_device(tokens, out_grad, gate_values, routing, gate_weight, up_weight, down_weight):
    width = tokens.shape[1]
    cut = lax.axis_index("cuts")
    x, c = cut // 2, cut % 2
    wg = jnp.swapaxes(gate_weight[0], 0, 1)
    wu = jnp.swapaxes(up_weight[0], 0, 1)
    w2 = down_weight[0]
    hidden = w2.shape[0]
    steps = jnp.arange(NX + 1)
    there = jnp.where(steps == 2, (x + 3 + 2 * (x % 2)) % NX, x ^ steps)
    there = jnp.where(steps == 3, x ^ 2, there)
    own_info = jnp.where(steps < NX, there * 2 + c, c)
    other_info = own_info ^ 1
    rows = NY * E * CAP

    select, weight = slots_of(routing, gate_values)
    pick = select.astype(BF).T
    send_x = jnp.dot(pick, tokens, preferred_element_type=F32).astype(BF)
    slot_gate = jnp.sum(weight, axis=0)
    send_dy = jnp.dot(pick, out_grad, preferred_element_type=F32)
    send_dy = (slot_gate[:, None] * send_dy).astype(BF)
    send = jnp.concatenate(
        [send_x.reshape(E, CAP, width), send_dy.reshape(E, CAP, width)], axis=1
    )
    got = swap_z(send).reshape(E, 2, CAP, width)
    got = jnp.swapaxes(got, 0, 1).reshape(2, E * CAP, width)

    parts = gather(got, 0)
    token = to_core(parts[3][0, :8, :128])[0, 0]
    near = jnp.where(token == token, jnp.stack(parts), jnp.zeros((), BF))
    weights = [pltpu.with_memory_space_constraint(w, pltpu.HBM) for w in (wg, wu, w2)]
    infos, near = lax.optimization_barrier((jnp.stack([own_info, other_info]), near))
    bufs = load_weights(infos, weights, width)
    own, bufs = lax.optimization_barrier((tuple(gather(near, 1)), tuple(bufs)))
    other = [to_core(v) for v in own]

    pre = jax.ShapeDtypeStruct((3 * hidden, rows), F32)
    act = [
        jax.ShapeDtypeStruct((rows, hidden), BF),
        jax.ShapeDtypeStruct((rows, 2 * hidden), BF),
    ]
    pieces = [jax.ShapeDtypeStruct((4, 4, 2, rows // 4, width), BF)]
    row_buf = [pltpu.VMEM((NX, 2, rows, width), BF)]
    acc_buf = [pltpu.VMEM(pre.shape, F32)]
    shape = rows, hidden, width
    (partial,) = call(
        own_kernel, "own", own_info, [*own, bufs[0]], [pre], row_buf, 3, shape
    )
    far, *act = call(
        other_kernel, "other", other_info, [*other, bufs[1], partial],
        pieces + act, row_buf + acc_buf, 6, shape,
    )
    (near,) = call(
        last_kernel, "last", own_info, [*act, bufs[0]], pieces, [], 3, shape
    )
    got = to_core(far)
    sums = scatter([add(near[b], got[b]) for b in range(4)], 1)
    back = scatter([sums[a] for a in range(4)], 0)
    back = back.reshape(2, E, CAP, width)
    back = jnp.swapaxes(back, 0, 1).reshape(E, 2 * CAP, width)
    back = swap_z(back)
    back_y = back[:, :CAP].reshape(E * CAP, width)
    back_dx = back[:, CAP:].reshape(E * CAP, width)
    mixed = jnp.dot(weight, back_y.astype(F32), precision=lax.Precision.HIGHEST)
    grad = jnp.dot(select.astype(BF), back_dx, preferred_element_type=F32)
    return mixed.astype(BF), grad.astype(BF)


def solution(mesh):
    return jax.shard_map(
        on_device,
        mesh=mesh,
        in_specs=(
            P("dp", "cuts"),
            P("dp", "cuts"),
            P("dp", None),
            P("dp", None),
            P("dp", None, "cuts"),
            P("dp", None, "cuts"),
            P("dp", "cuts", None),
        ),
        out_specs=(P("dp", "cuts"), P("dp", "cuts")),
        check_vma=False,
    )
```

```python
import itertools

import jax
import jax.numpy as jnp
from jax import lax
from jax.experimental import pallas as pl
from jax.experimental.pallas import tpu as pltpu
from jax.sharding import PartitionSpec as P

E = 8
NY = 4
NX = 4
CAP = 8
TOPK = 2
BF = jnp.bfloat16
F32 = jnp.float32
NT = (((1,), (1,)), ((), ()))
VMEM_LIMIT = {"own": 8, "other": 12, "last": 4}


Z_GROUPS = [[z * NY + y for z in range(E)] for y in range(NY)]


def gather_z(v):
    return lax.all_gather(v, "dp", axis_index_groups=Z_GROUPS)


def swap_z(v):
    return lax.all_to_all(v, "dp", 0, 0, axis_index_groups=Z_GROUPS, tiled=True)


def partner(i, q):
    if q == 1:
        return i ^ 1
    return (i + (1 if i % 2 else 3)) % 4 if q == 2 else i ^ 2


def swap(v, q, along_y):
    def place(z, y, x, c):
        return (z * NY + y) * 2 * NX + x * 2 + c

    perm = []
    for z, y, x, c in itertools.product(range(E), range(NY), range(NX), range(2)):
        if c == along_y:
            to = place(z, partner(y, q), x, c)
        else:
            to = place(z, y, partner(x, q), c)
        perm.append((place(z, y, x, c), to))
    return lax.ppermute(v, ("dp", "cuts"), perm)


def to_core(v):
    return lax.ppermute(v, "cuts", [(i, i ^ 1) for i in range(2 * NX)])


def thirds(v):
    first = v.astype(BF)
    rest = v - first.astype(F32)
    second = rest.astype(BF)
    return first, second, (rest - second.astype(F32)).astype(BF)


def later(n):
    i = lax.broadcasted_iota(jnp.int32, (n, n), 0)
    j = lax.broadcasted_iota(jnp.int32, (n, n), 1)
    return jnp.where(i < j, 1.0, 0.0).astype(BF)


def pack_kernel(tokens, out_grad, routing_in, gates_in, out, routing, gates, sem):
    rows = tokens.shape[0]
    copies = [
        pltpu.make_async_copy(tokens, out.at[:rows], sem.at[0]),
        pltpu.make_async_copy(out_grad, out.at[rows : 2 * rows], sem.at[1]),
        pltpu.make_async_copy(routing_in, routing, sem.at[2]),
        pltpu.make_async_copy(gates_in, gates, sem.at[3]),
    ]
    for copy in copies:
        copy.start()
    out[2 * rows :] = jnp.zeros_like(out[2 * rows :])
    copies[2].wait()
    copies[3].wait()
    info = [routing[k : k + 1, :].astype(F32) for k in range(TOPK)]
    for k in range(TOPK):
        info += [p.astype(F32) for p in thirds(gates[k : k + 1, :])]
    out[2 * rows :, :rows] = jnp.concatenate(info, axis=0).astype(BF)
    copies[0].wait()
    copies[1].wait()


def slot_kernel(expert, got, out):
    rows = (got.shape[1] - 8) // 2
    e = expert[0].astype(F32)
    lanes = 128
    lane = lax.broadcasted_iota(jnp.int32, (CAP, lanes), 1)
    slot = lax.broadcasted_iota(jnp.int32, (CAP, lanes), 0).astype(F32)
    before = later(lanes)
    xs, dys = [], []
    for z in range(E):
        info = got[z, 2 * rows :, :lanes].astype(F32)
        is0 = info[0:1] == e
        chosen = (is0 | (info[1:2] == e)) & (lane < rows)
        flags = jnp.where(chosen, 1.0, 0.0).astype(BF)
        position = jnp.dot(flags, before, preferred_element_type=F32)
        select = chosen & (position == slot)
        gate0 = info[2:3] + info[3:4] + info[4:5]
        gate1 = info[5:6] + info[6:7] + info[7:8]
        gate = jnp.where(is0, gate0, gate1)
        gate = jnp.sum(jnp.where(select, gate, 0.0), axis=1, keepdims=True)
        pick = jnp.where(select, 1.0, 0.0)[:, :rows].astype(BF)
        xs.append(jnp.dot(pick, got[z, :rows], preferred_element_type=F32))
        dy = jnp.dot(pick, got[z, rows : 2 * rows], preferred_element_type=F32)
        dys.append(gate * dy)
    out[0] = jnp.concatenate(xs, axis=0).astype(BF)
    out[1] = jnp.concatenate(dys, axis=0).astype(BF)


def own_slots(routing, gates, mix, select_ref):
    rows = routing.shape[1]
    shape = E * CAP, rows
    index = lax.broadcasted_iota(jnp.int32, shape, 0)
    expert = index // CAP
    is0 = routing[0:1, :] == expert
    chosen = is0 | (routing[1:2, :] == expert)
    flags = jnp.where(chosen, 1.0, 0.0).astype(BF)
    position = jnp.dot(flags, later(rows), preferred_element_type=F32)
    select = chosen & (position == (index % CAP).astype(F32))
    gate = jnp.where(is0, gates[0:1, :], gates[1:2, :])
    i = lax.broadcasted_iota(jnp.int32, (rows, rows), 0)
    j = lax.broadcasted_iota(jnp.int32, (rows, rows), 1)
    eye = jnp.where(i == j, 1.0, 0.0).astype(BF)

    def turned(v):
        return lax.dot_general(eye, v, NT, preferred_element_type=F32).astype(BF)

    select_ref[...] = turned(jnp.where(select, 1.0, 0.0).astype(BF))
    for n, part in enumerate(thirds(jnp.where(select, gate, 0.0))):
        mix[n] = turned(part)


def combine_kernel(back, mix, select, mixed, grad):
    def rows(at):
        parts = [back[e, at : at + CAP].astype(F32) for e in range(E)]
        return jnp.concatenate(parts, axis=0).astype(BF)

    y, dx = rows(0), rows(CAP)
    total = jnp.dot(mix[0], y, preferred_element_type=F32)
    for n in (1, 2):
        total = total + jnp.dot(mix[n], y, preferred_element_type=F32)
    mixed[...] = total.astype(BF)
    grad[...] = jnp.dot(select[...], dx, preferred_element_type=F32).astype(BF)


def small(body, name, out, arrays, scalars=0):
    return pl.pallas_call(
        body,
        name=name,
        out_shape=out,
        in_specs=[pl.BlockSpec(memory_space=pltpu.SMEM)] * scalars
        + [pl.BlockSpec(memory_space=pltpu.VMEM)] * (len(arrays) - scalars),
        out_specs=jax.tree.map(lambda _: pl.BlockSpec(memory_space=pltpu.VMEM), out),
        compiler_params=pltpu.CompilerParams(vmem_limit_bytes=4 << 20),
    )(*arrays)


def gather(v, along_y):
    far, near, next_ = lax.optimization_barrier(
        tuple(swap(v, q, along_y) for q in (3, 1, 2))
    )
    return [v, near, next_, far]


def add(*parts):
    total = parts[0].astype(F32)
    for p in parts[1:]:
        total = total + p.astype(F32)
    return total.astype(BF)


def scatter(parts, along_y):
    parts = lax.optimization_barrier(tuple(parts))
    got = lax.optimization_barrier(
        tuple(swap(parts[q], q, along_y) for q in (3, 1, 2))
    )
    return add(parts[0], *got)


def weights_kernel(infos, routing, gates, *refs):
    weights, bufs, mix, select, sem = refs[:3], refs[3:5], refs[5], refs[6], refs[7]
    hidden, width = weights[0].shape[0], bufs[0].shape[-1]
    copies = []
    for core in range(2):
        for k in range(NX):
            at = pl.ds(pl.multiple_of(infos[core, k] * width, 128), width)
            for i in range(3):
                to = bufs[core].at[k, pl.ds(i * hidden, hidden)]
                copies.append(
                    pltpu.make_async_copy(
                        weights[i].at[:, at], to, sem.at[core, k, i]
                    )
                )
    for copy in copies:
        copy.start()
    own_slots(routing, gates, mix, select)
    for copy in copies:
        copy.wait()


def load_weights(infos, routing, gates, weights, width):
    hidden = weights[0].shape[0]
    return pl.pallas_call(
        weights_kernel,
        name="weights",
        out_shape=[jax.ShapeDtypeStruct((NX, 3 * hidden, width), BF)] * 2
        + [
            jax.ShapeDtypeStruct((3, routing.shape[1], E * CAP), BF),
            jax.ShapeDtypeStruct((routing.shape[1], E * CAP), BF),
        ],
        in_specs=[pl.BlockSpec(memory_space=pltpu.SMEM)]
        + [pl.BlockSpec(memory_space=pltpu.VMEM)] * 2
        + [pl.BlockSpec(memory_space=pltpu.HBM)] * 3,
        out_specs=[pl.BlockSpec(memory_space=pltpu.VMEM)] * 4,
        scratch_shapes=[pltpu.SemaphoreType.DMA((2, NX, 3))],
        compiler_params=pltpu.CompilerParams(vmem_limit_bytes=4 << 20),
        cost_estimate=pl.CostEstimate(
            flops=0, bytes_accessed=26 << 20, transcendentals=0
        ),
    )(infos, routing, gates, *weights)


def order(info, b, a):
    first = info[NX] == 0
    return jnp.where(first, b, a), jnp.where(first, a, b)


def load_rows(info, pieces, rows):
    step = rows.shape[2] // NY
    for b in range(4):
        for a in range(4):
            k, j = order(info, b, a)
            at = pl.ds(pl.multiple_of(j * step, step), step)
            for i in range(2):
                rows[k, i, at] = pieces[b][a, i]


def contract(rows, buf, acc):
    two = acc.shape[0] // 3 * 2

    @pl.loop(0, NX)
    def _(k):
        acc[:two] += lax.dot_general(
            buf[k, :two], rows[k, 0], NT, preferred_element_type=F32
        )
        acc[two:] += lax.dot_general(
            buf[k, two:], rows[k, 1], NT, preferred_element_type=F32
        )


def expand(info, hidden, grads, buf, out):
    step = hidden.shape[0] // NY
    two = grads.shape[1]

    def put(k, i, value):
        for j in range(NY):
            b, a = order(info, k, j)
            out[b, a, i] = value[j * step : (j + 1) * step]

    @pl.loop(0, NX)
    def _(k):
        o = jnp.dot(hidden[...], buf[k, two:], preferred_element_type=F32)
        put(k, 0, o.astype(BF))
        o = jnp.dot(grads[...], buf[k, :two], preferred_element_type=F32)
        put(k, 1, o.astype(BF))


def own_kernel(info, *refs):
    pieces, (buf, acc, rows) = refs[:4], refs[4:]
    load_rows(info, pieces, rows)
    acc[...] = jnp.zeros_like(acc)
    contract(rows, buf, acc)


def other_kernel(info, *refs):
    pieces, (buf, partial, out, hidden, grads, rows, acc) = refs[:4], refs[4:]
    load_rows(info, pieces, rows)
    acc[...] = partial[...]
    contract(rows, buf, acc)
    one = acc.shape[0] // 3
    g, u, h = acc[:one], acc[one : 2 * one], acc[2 * one :]
    sigma = jax.nn.sigmoid(g)
    hidden[...] = (g * sigma * u).T.astype(BF)
    gate_grad = h * u * sigma * (1.0 + g * (1.0 - sigma))
    grads[...] = jnp.concatenate([gate_grad, h * g * sigma], axis=0).T.astype(BF)
    expand(info, hidden, grads, buf, out)


def last_kernel(info, hidden, grads, buf, out):
    expand(info, hidden, grads, buf, out)


def call(body, name, info, arrays, out, scratch, products, shape):
    rows, hidden, width = shape
    return pl.pallas_call(
        body,
        name=name,
        out_shape=out,
        in_specs=[pl.BlockSpec(memory_space=pltpu.SMEM)]
        + [pl.BlockSpec(memory_space=pltpu.VMEM)] * len(arrays),
        out_specs=[pl.BlockSpec(memory_space=pltpu.VMEM)] * len(out),
        scratch_shapes=scratch,
        compiler_params=pltpu.CompilerParams(vmem_limit_bytes=VMEM_LIMIT[name] << 20),
        cost_estimate=pl.CostEstimate(
            flops=2 * products * rows * width * NX * hidden,
            bytes_accessed=7 << 20,
            transcendentals=0,
        ),
    )(info, *arrays)


def on_device(tokens, out_grad, gate_values, routing, gate_weight, up_weight, down_weight):
    width = tokens.shape[1]
    cut = lax.axis_index("cuts")
    x, c = cut // 2, cut % 2
    wg = jnp.swapaxes(gate_weight[0], 0, 1)
    wu = jnp.swapaxes(up_weight[0], 0, 1)
    w2 = down_weight[0]
    hidden = w2.shape[0]
    steps = jnp.arange(NX + 1)
    there = jnp.where(steps == 2, (x + 3 + 2 * (x % 2)) % NX, x ^ steps)
    there = jnp.where(steps == 3, x ^ 2, there)
    own_info = jnp.where(steps < NX, there * 2 + c, c)
    other_info = own_info ^ 1
    rows = NY * E * CAP

    turned = jnp.swapaxes(routing, 0, 1), jnp.swapaxes(gate_values, 0, 1)
    packed = jax.ShapeDtypeStruct((2 * tokens.shape[0] + 8, width), BF)
    packed = pl.pallas_call(
        pack_kernel,
        name="pack",
        out_shape=packed,
        in_specs=[pl.BlockSpec(memory_space=pl.ANY)] * 4,
        out_specs=pl.BlockSpec(memory_space=pltpu.VMEM),
        scratch_shapes=[
            pltpu.VMEM(turned[0].shape, jnp.int32),
            pltpu.VMEM(turned[1].shape, F32),
            pltpu.SemaphoreType.DMA((4,)),
        ],
    )(
        *[
            pltpu.with_memory_space_constraint(v, pltpu.HBM)
            for v in (tokens, out_grad, *turned)
        ]
    )
    plane = (lax.axis_index("dp") // NY).reshape(1)
    got = jax.ShapeDtypeStruct((2, E * CAP, width), BF)
    got = small(slot_kernel, "slots", got, [plane, gather_z(packed)], 1)

    parts = gather(got, 0)
    token = to_core(parts[3][0, :8])[0]
    near = jnp.where(token == token, jnp.stack(parts), jnp.zeros((), BF))
    weights = [pltpu.with_memory_space_constraint(w, pltpu.HBM) for w in (wg, wu, w2)]
    infos, near = lax.optimization_barrier((jnp.stack([own_info, other_info]), near))
    bufs = load_weights(infos, *turned, weights, width)
    own, bufs = lax.optimization_barrier((tuple(gather(near, 1)), tuple(bufs)))
    other = [to_core(v) for v in own]

    pre = jax.ShapeDtypeStruct((3 * hidden, rows), F32)
    act = [
        jax.ShapeDtypeStruct((rows, hidden), BF),
        jax.ShapeDtypeStruct((rows, 2 * hidden), BF),
    ]
    pieces = [jax.ShapeDtypeStruct((4, 4, 2, rows // 4, width), BF)]
    row_buf = [pltpu.VMEM((NX, 2, rows, width), BF)]
    acc_buf = [pltpu.VMEM(pre.shape, F32)]
    shape = rows, hidden, width
    (partial,) = call(
        own_kernel, "own", own_info, [*own, bufs[0]], [pre], row_buf, 3, shape
    )
    far, *act = call(
        other_kernel, "other", other_info, [*other, bufs[1], partial],
        pieces + act, row_buf + acc_buf, 6, shape,
    )
    (near,) = call(
        last_kernel, "last", own_info, [*act, bufs[0]], pieces, [], 3, shape
    )
    got = to_core(far)
    sums = scatter([add(near[b], got[b]) for b in range(4)], 1)
    back = scatter([sums[a] for a in range(4)], 0)
    back = back.reshape(2, E, CAP, width)
    back = jnp.swapaxes(back, 0, 1).reshape(E, 2 * CAP, width)
    back = swap_z(back)
    result = [jax.ShapeDtypeStruct(tokens.shape, BF)] * 2
    return tuple(small(combine_kernel, "combine", result, [back, bufs[2], bufs[3]]))


def solution(mesh):
    return jax.shard_map(
        on_device,
        mesh=mesh,
        in_specs=(
            P("dp", "cuts"),
            P("dp", "cuts"),
            P("dp", None),
            P("dp", None),
            P("dp", None, "cuts"),
            P("dp", None, "cuts"),
            P("dp", "cuts", None),
        ),
        out_specs=(P("dp", "cuts"), P("dp", "cuts")),
        check_vma=False,
    )
```

```python
import itertools

import jax
import jax.numpy as jnp
from jax import lax
from jax.experimental import pallas as pl
from jax.experimental.pallas import tpu as pltpu
from jax.sharding import PartitionSpec as P

E = 8
NY = 4
NX = 4
CAP = 8
TOPK = 2
BF = jnp.bfloat16
F32 = jnp.float32
NT = (((1,), (1,)), ((), ()))
VMEM_LIMIT = {"own": 8, "other": 12, "last": 4}


Z_GROUPS = [[z * NY + y for z in range(E)] for y in range(NY)]


def swap_z(v):
    return lax.all_to_all(v, "dp", 0, 0, axis_index_groups=Z_GROUPS, tiled=True)


def partner(i, q):
    if q == 1:
        return i ^ 1
    return (i + (1 if i % 2 else 3)) % 4 if q == 2 else i ^ 2


def swap(v, q, along_y):
    def place(z, y, x, c):
        return (z * NY + y) * 2 * NX + x * 2 + c

    perm = []
    for z, y, x, c in itertools.product(range(E), range(NY), range(NX), range(2)):
        if c == along_y:
            to = place(z, partner(y, q), x, c)
        else:
            to = place(z, y, partner(x, q), c)
        perm.append((place(z, y, x, c), to))
    return lax.ppermute(v, ("dp", "cuts"), perm)


def to_core(v):
    return lax.ppermute(v, "cuts", [(i, i ^ 1) for i in range(2 * NX)])


def thirds(v):
    first = v.astype(BF)
    rest = v - first.astype(F32)
    second = rest.astype(BF)
    return first, second, (rest - second.astype(F32)).astype(BF)


def later(n):
    i = lax.broadcasted_iota(jnp.int32, (n, n), 0)
    j = lax.broadcasted_iota(jnp.int32, (n, n), 1)
    return jnp.where(i < j, 1.0, 0.0).astype(BF)


def choose(routing, gates):
    shape = E * CAP, routing.shape[1]
    index = lax.broadcasted_iota(jnp.int32, shape, 0)
    expert = index // CAP
    is0 = routing[0:1, :] == expert
    chosen = is0 | (routing[1:2, :] == expert)
    flags = jnp.where(chosen, 1.0, 0.0).astype(BF)
    position = jnp.dot(flags, later(shape[1]), preferred_element_type=F32)
    select = chosen & (position == (index % CAP).astype(F32))
    return select, jnp.where(is0, gates[0:1, :], gates[1:2, :])


def send_kernel(tokens_in, dy_in, routing_in, gates_in, out, tokens, dy, routing, gates, sem):
    pairs = (routing_in, routing), (gates_in, gates), (tokens_in, tokens), (dy_in, dy)
    copies = [
        pltpu.make_async_copy(a, b, sem.at[n]) for n, (a, b) in enumerate(pairs)
    ]
    for copy in copies:
        copy.start()
    copies[0].wait()
    copies[1].wait()
    select, gate = choose(routing, gates)
    gate = jnp.sum(jnp.where(select, gate, 0.0), axis=1, keepdims=True)
    pick = jnp.where(select, 1.0, 0.0).astype(BF)
    copies[2].wait()
    copies[3].wait()
    x = jnp.dot(pick, tokens[...], preferred_element_type=F32)
    grad = gate * jnp.dot(pick, dy[...], preferred_element_type=F32)
    for e in range(E):
        at = slice(e * CAP, (e + 1) * CAP)
        out[e] = jnp.concatenate([x[at], grad[at]], axis=0).astype(BF)


def own_slots(routing, gates, mix, select_ref):
    rows = routing.shape[1]
    select, gate = choose(routing, gates)
    i = lax.broadcasted_iota(jnp.int32, (rows, rows), 0)
    j = lax.broadcasted_iota(jnp.int32, (rows, rows), 1)
    eye = jnp.where(i == j, 1.0, 0.0).astype(BF)

    def turned(v):
        return lax.dot_general(eye, v, NT, preferred_element_type=F32).astype(BF)

    select_ref[...] = turned(jnp.where(select, 1.0, 0.0).astype(BF))
    for n, part in enumerate(thirds(jnp.where(select, gate, 0.0))):
        mix[n] = turned(part)


def combine_kernel(back, mix, select, mixed, grad):
    def rows(at):
        parts = [back[e, at : at + CAP].astype(F32) for e in range(E)]
        return jnp.concatenate(parts, axis=0).astype(BF)

    y, dx = rows(0), rows(CAP)
    total = jnp.dot(mix[0], y, preferred_element_type=F32)
    for n in (1, 2):
        total = total + jnp.dot(mix[n], y, preferred_element_type=F32)
    mixed[...] = total.astype(BF)
    grad[...] = jnp.dot(select[...], dx, preferred_element_type=F32).astype(BF)


def small(body, name, out, arrays, scalars=0):
    return pl.pallas_call(
        body,
        name=name,
        out_shape=out,
        in_specs=[pl.BlockSpec(memory_space=pltpu.SMEM)] * scalars
        + [pl.BlockSpec(memory_space=pltpu.VMEM)] * (len(arrays) - scalars),
        out_specs=jax.tree.map(lambda _: pl.BlockSpec(memory_space=pltpu.VMEM), out),
        compiler_params=pltpu.CompilerParams(vmem_limit_bytes=4 << 20),
    )(*arrays)


def gather(v, along_y):
    far, near, next_ = lax.optimization_barrier(
        tuple(swap(v, q, along_y) for q in (3, 1, 2))
    )
    return [v, near, next_, far]


def add(*parts):
    total = parts[0].astype(F32)
    for p in parts[1:]:
        total = total + p.astype(F32)
    return total.astype(BF)


def scatter(parts, along_y):
    parts = lax.optimization_barrier(tuple(parts))
    got = lax.optimization_barrier(
        tuple(swap(parts[q], q, along_y) for q in (3, 1, 2))
    )
    return add(parts[0], *got)


def weights_kernel(infos, routing, gates, *refs):
    weights, bufs, mix, select, sem = refs[:3], refs[3:5], refs[5], refs[6], refs[7]
    hidden, width = weights[0].shape[0], bufs[0].shape[-1]
    copies = []
    for core in range(2):
        for k in range(NX):
            at = pl.ds(pl.multiple_of(infos[core, k] * width, 128), width)
            for i in range(3):
                to = bufs[core].at[k, pl.ds(i * hidden, hidden)]
                copies.append(
                    pltpu.make_async_copy(
                        weights[i].at[:, at], to, sem.at[core, k, i]
                    )
                )
    for copy in copies:
        copy.start()
    own_slots(routing, gates, mix, select)
    for copy in copies:
        copy.wait()


def load_weights(infos, routing, gates, weights, width):
    hidden = weights[0].shape[0]
    return pl.pallas_call(
        weights_kernel,
        name="weights",
        out_shape=[jax.ShapeDtypeStruct((NX, 3 * hidden, width), BF)] * 2
        + [
            jax.ShapeDtypeStruct((3, routing.shape[1], E * CAP), BF),
            jax.ShapeDtypeStruct((routing.shape[1], E * CAP), BF),
        ],
        in_specs=[pl.BlockSpec(memory_space=pltpu.SMEM)]
        + [pl.BlockSpec(memory_space=pltpu.VMEM)] * 2
        + [pl.BlockSpec(memory_space=pltpu.HBM)] * 3,
        out_specs=[pl.BlockSpec(memory_space=pltpu.VMEM)] * 4,
        scratch_shapes=[pltpu.SemaphoreType.DMA((2, NX, 3))],
        compiler_params=pltpu.CompilerParams(vmem_limit_bytes=4 << 20),
        cost_estimate=pl.CostEstimate(
            flops=0, bytes_accessed=26 << 20, transcendentals=0
        ),
    )(infos, routing, gates, *weights)


def order(info, b, a):
    first = info[NX] == 0
    return jnp.where(first, b, a), jnp.where(first, a, b)


def load_rows(info, pieces, rows):
    step = rows.shape[2] // NY
    for b in range(4):
        for a in range(4):
            k, j = order(info, b, a)
            at = pl.ds(pl.multiple_of(j * step, step), step)
            for i in range(2):
                rows[k, i, at] = pieces[b][a, i]


def contract(rows, buf, acc):
    two = acc.shape[0] // 3 * 2

    @pl.loop(0, NX)
    def _(k):
        acc[:two] += lax.dot_general(
            buf[k, :two], rows[k, 0], NT, preferred_element_type=F32
        )
        acc[two:] += lax.dot_general(
            buf[k, two:], rows[k, 1], NT, preferred_element_type=F32
        )


def expand(info, hidden, grads, buf, out):
    step = hidden.shape[0] // NY
    two = grads.shape[1]

    def put(k, i, value):
        for j in range(NY):
            b, a = order(info, k, j)
            out[b, a, i] = value[j * step : (j + 1) * step]

    @pl.loop(0, NX)
    def _(k):
        o = jnp.dot(hidden[...], buf[k, two:], preferred_element_type=F32)
        put(k, 0, o.astype(BF))
        o = jnp.dot(grads[...], buf[k, :two], preferred_element_type=F32)
        put(k, 1, o.astype(BF))


def own_kernel(info, *refs):
    pieces, (buf, acc, rows) = refs[:4], refs[4:]
    load_rows(info, pieces, rows)
    acc[...] = jnp.zeros_like(acc)
    contract(rows, buf, acc)


def other_kernel(info, *refs):
    pieces, (buf, partial, out, hidden, grads, rows, acc) = refs[:4], refs[4:]
    load_rows(info, pieces, rows)
    acc[...] = partial[...]
    contract(rows, buf, acc)
    one = acc.shape[0] // 3
    g, u, h = acc[:one], acc[one : 2 * one], acc[2 * one :]
    sigma = jax.nn.sigmoid(g)
    hidden[...] = (g * sigma * u).T.astype(BF)
    gate_grad = h * u * sigma * (1.0 + g * (1.0 - sigma))
    grads[...] = jnp.concatenate([gate_grad, h * g * sigma], axis=0).T.astype(BF)
    expand(info, hidden, grads, buf, out)


def last_kernel(info, hidden, grads, buf, out):
    expand(info, hidden, grads, buf, out)


def call(body, name, info, arrays, out, scratch, products, shape):
    rows, hidden, width = shape
    return pl.pallas_call(
        body,
        name=name,
        out_shape=out,
        in_specs=[pl.BlockSpec(memory_space=pltpu.SMEM)]
        + [pl.BlockSpec(memory_space=pltpu.VMEM)] * len(arrays),
        out_specs=[pl.BlockSpec(memory_space=pltpu.VMEM)] * len(out),
        scratch_shapes=scratch,
        compiler_params=pltpu.CompilerParams(vmem_limit_bytes=VMEM_LIMIT[name] << 20),
        cost_estimate=pl.CostEstimate(
            flops=2 * products * rows * width * NX * hidden,
            bytes_accessed=7 << 20,
            transcendentals=0,
        ),
    )(info, *arrays)


def on_device(tokens, out_grad, gate_values, routing, gate_weight, up_weight, down_weight):
    width = tokens.shape[1]
    cut = lax.axis_index("cuts")
    x, c = cut // 2, cut % 2
    wg = jnp.swapaxes(gate_weight[0], 0, 1)
    wu = jnp.swapaxes(up_weight[0], 0, 1)
    w2 = down_weight[0]
    hidden = w2.shape[0]
    steps = jnp.arange(NX + 1)
    there = jnp.where(steps == 2, (x + 3 + 2 * (x % 2)) % NX, x ^ steps)
    there = jnp.where(steps == 3, x ^ 2, there)
    own_info = jnp.where(steps < NX, there * 2 + c, c)
    other_info = own_info ^ 1
    rows = NY * E * CAP

    turned = jnp.swapaxes(routing, 0, 1), jnp.swapaxes(gate_values, 0, 1)
    sources = tokens, out_grad, *turned
    send = pl.pallas_call(
        send_kernel,
        name="send",
        out_shape=jax.ShapeDtypeStruct((E, 2 * CAP, width), BF),
        in_specs=[pl.BlockSpec(memory_space=pl.ANY)] * 4,
        out_specs=pl.BlockSpec(memory_space=pltpu.VMEM),
        scratch_shapes=[pltpu.VMEM(v.shape, v.dtype) for v in sources]
        + [pltpu.SemaphoreType.DMA((4,))],
    )(*[pltpu.with_memory_space_constraint(v, pltpu.HBM) for v in sources])
    got = swap_z(send).reshape(E, 2, CAP, width)
    got = jnp.swapaxes(got, 0, 1).reshape(2, E * CAP, width)

    parts = gather(got, 0)
    token = to_core(parts[3][0, :8])[0]
    near = jnp.where(token == token, jnp.stack(parts), jnp.zeros((), BF))
    weights = [pltpu.with_memory_space_constraint(w, pltpu.HBM) for w in (wg, wu, w2)]
    infos, near = lax.optimization_barrier((jnp.stack([own_info, other_info]), near))
    bufs = load_weights(infos, *turned, weights, width)
    third, first, second = (swap(near, q, 1) for q in (3, 1, 2))
    other = tuple(to_core(v) for v in (near, first, second))
    third, other, bufs = lax.optimization_barrier((third, other, tuple(bufs)))
    other = [*other, to_core(third)]
    own = [near, first, second, third]

    pre = jax.ShapeDtypeStruct((3 * hidden, rows), F32)
    act = [
        jax.ShapeDtypeStruct((rows, hidden), BF),
        jax.ShapeDtypeStruct((rows, 2 * hidden), BF),
    ]
    pieces = [jax.ShapeDtypeStruct((4, 4, 2, rows // 4, width), BF)]
    row_buf = [pltpu.VMEM((NX, 2, rows, width), BF)]
    acc_buf = [pltpu.VMEM(pre.shape, F32)]
    shape = rows, hidden, width
    (partial,) = call(
        own_kernel, "own", own_info, [*own, bufs[0]], [pre], row_buf, 3, shape
    )
    far, *act = call(
        other_kernel, "other", other_info, [*other, bufs[1], partial],
        pieces + act, row_buf + acc_buf, 6, shape,
    )
    (near,) = call(
        last_kernel, "last", own_info, [*act, bufs[0]], pieces, [], 3, shape
    )
    got = to_core(far)
    sums = scatter([add(near[b], got[b]) for b in range(4)], 1)
    back = scatter([sums[a] for a in range(4)], 0)
    back = back.reshape(2, E, CAP, width)
    back = jnp.swapaxes(back, 0, 1).reshape(E, 2 * CAP, width)
    back = swap_z(back)
    result = [jax.ShapeDtypeStruct(tokens.shape, BF)] * 2
    return tuple(small(combine_kernel, "combine", result, [back, bufs[2], bufs[3]]))


def solution(mesh):
    return jax.shard_map(
        on_device,
        mesh=mesh,
        in_specs=(
            P("dp", "cuts"),
            P("dp", "cuts"),
            P("dp", None),
            P("dp", None),
            P("dp", None, "cuts"),
            P("dp", None, "cuts"),
            P("dp", "cuts", None),
        ),
        out_specs=(P("dp", "cuts"), P("dp", "cuts")),
        check_vma=False,
    )
```

```python
import itertools

import jax
import jax.numpy as jnp
from jax import lax
from jax.experimental import pallas as pl
from jax.experimental.pallas import tpu as pltpu
from jax.sharding import PartitionSpec as P

E = 8
NY = 4
NX = 4
CAP = 8
TOPK = 2
BF = jnp.bfloat16
F32 = jnp.float32
NT = (((1,), (1,)), ((), ()))
VMEM_LIMIT = {"own": 8, "other": 12, "last": 4}


Z_GROUPS = [[z * NY + y for z in reversed(range(E))] for y in range(NY)]


def swap_z(v):
    return lax.all_to_all(v, "dp", 0, 0, axis_index_groups=Z_GROUPS, tiled=True)


def partner(i, q):
    if q == 1:
        return i ^ 1
    return (i + (1 if i % 2 else 3)) % 4 if q == 2 else i ^ 2


def swap(v, q, along_y):
    def place(z, y, x, c):
        return (z * NY + y) * 2 * NX + x * 2 + c

    perm = []
    for z, y, x, c in itertools.product(range(E), range(NY), range(NX), range(2)):
        if c == along_y:
            to = place(z, partner(y, q), x, c)
        else:
            to = place(z, y, partner(x, q), c)
        perm.append((place(z, y, x, c), to))
    return lax.ppermute(v, ("dp", "cuts"), perm)


def to_core(v):
    return lax.ppermute(v, "cuts", [(i, i ^ 1) for i in range(2 * NX)])


def thirds(v):
    first = v.astype(BF)
    rest = v - first.astype(F32)
    second = rest.astype(BF)
    return first, second, (rest - second.astype(F32)).astype(BF)


def later(n):
    i = lax.broadcasted_iota(jnp.int32, (n, n), 0)
    j = lax.broadcasted_iota(jnp.int32, (n, n), 1)
    return jnp.where(i < j, 1.0, 0.0).astype(BF)


def choose(routing, gates):
    shape = E * CAP, routing.shape[1]
    index = lax.broadcasted_iota(jnp.int32, shape, 0)
    expert = index // CAP
    is0 = routing[0:1, :] == expert
    chosen = is0 | (routing[1:2, :] == expert)
    flags = jnp.where(chosen, 1.0, 0.0).astype(BF)
    position = jnp.dot(flags, later(shape[1]), preferred_element_type=F32)
    select = chosen & (position == (index % CAP).astype(F32))
    return select, jnp.where(is0, gates[0:1, :], gates[1:2, :])


def send_kernel(tokens_in, dy_in, routing_in, gates_in, out, tokens, dy, routing, gates, sem):
    pairs = (routing_in, routing), (gates_in, gates), (tokens_in, tokens), (dy_in, dy)
    copies = [
        pltpu.make_async_copy(a, b, sem.at[n]) for n, (a, b) in enumerate(pairs)
    ]
    for copy in copies:
        copy.start()
    copies[0].wait()
    copies[1].wait()
    select, gate = choose(routing, gates)
    gate = jnp.sum(jnp.where(select, gate, 0.0), axis=1, keepdims=True)
    pick = jnp.where(select, 1.0, 0.0).astype(BF)
    copies[2].wait()
    copies[3].wait()
    x = jnp.dot(pick, tokens[...], preferred_element_type=F32)
    grad = gate * jnp.dot(pick, dy[...], preferred_element_type=F32)
    for e in range(E):
        at = slice(e * CAP, (e + 1) * CAP)
        out[E - 1 - e] = jnp.concatenate([x[at], grad[at]], axis=0).astype(BF)


def own_slots(routing, gates, mix, select_ref):
    rows = routing.shape[1]
    select, gate = choose(routing, gates)
    i = lax.broadcasted_iota(jnp.int32, (rows, rows), 0)
    j = lax.broadcasted_iota(jnp.int32, (rows, rows), 1)
    eye = jnp.where(i == j, 1.0, 0.0).astype(BF)

    def turned(v):
        return lax.dot_general(eye, v, NT, preferred_element_type=F32).astype(BF)

    select_ref[...] = turned(jnp.where(select, 1.0, 0.0).astype(BF))
    for n, part in enumerate(thirds(jnp.where(select, gate, 0.0))):
        mix[n] = turned(part)


def combine_kernel(back, mix, select, mixed, grad):
    def rows(at):
        parts = [back[E - 1 - e, at : at + CAP].astype(F32) for e in range(E)]
        return jnp.concatenate(parts, axis=0).astype(BF)

    y, dx = rows(0), rows(CAP)
    total = jnp.dot(mix[0], y, preferred_element_type=F32)
    for n in (1, 2):
        total = total + jnp.dot(mix[n], y, preferred_element_type=F32)
    mixed[...] = total.astype(BF)
    grad[...] = jnp.dot(select[...], dx, preferred_element_type=F32).astype(BF)


def small(body, name, out, arrays, scalars=0):
    return pl.pallas_call(
        body,
        name=name,
        out_shape=out,
        in_specs=[pl.BlockSpec(memory_space=pltpu.SMEM)] * scalars
        + [pl.BlockSpec(memory_space=pltpu.VMEM)] * (len(arrays) - scalars),
        out_specs=jax.tree.map(lambda _: pl.BlockSpec(memory_space=pltpu.VMEM), out),
        compiler_params=pltpu.CompilerParams(vmem_limit_bytes=4 << 20),
    )(*arrays)


def gather(v, along_y):
    far, near, next_ = lax.optimization_barrier(
        tuple(swap(v, q, along_y) for q in (3, 1, 2))
    )
    return [v, near, next_, far]


def add(*parts):
    total = parts[0].astype(F32)
    for p in parts[1:]:
        total = total + p.astype(F32)
    return total.astype(BF)


def scatter(parts, along_y):
    parts = lax.optimization_barrier(tuple(parts))
    got = lax.optimization_barrier(
        tuple(swap(parts[q], q, along_y) for q in (3, 1, 2))
    )
    return add(parts[0], *got)


def weights_kernel(infos, routing, gates, *refs):
    weights, bufs, mix, select, sem = refs[:3], refs[3:5], refs[5], refs[6], refs[7]
    hidden, width = weights[0].shape[0], bufs[0].shape[-1]
    copies = []
    for core in range(2):
        for k in range(NX):
            at = pl.ds(pl.multiple_of(infos[core, k] * width, 128), width)
            for i in range(3):
                to = bufs[core].at[k, pl.ds(i * hidden, hidden)]
                copies.append(
                    pltpu.make_async_copy(
                        weights[i].at[:, at], to, sem.at[core, k, i]
                    )
                )
    for copy in copies:
        copy.start()
    own_slots(routing, gates, mix, select)
    for copy in copies:
        copy.wait()


def load_weights(infos, routing, gates, weights, width):
    hidden = weights[0].shape[0]
    return pl.pallas_call(
        weights_kernel,
        name="weights",
        out_shape=[jax.ShapeDtypeStruct((NX, 3 * hidden, width), BF)] * 2
        + [
            jax.ShapeDtypeStruct((3, routing.shape[1], E * CAP), BF),
            jax.ShapeDtypeStruct((routing.shape[1], E * CAP), BF),
        ],
        in_specs=[pl.BlockSpec(memory_space=pltpu.SMEM)]
        + [pl.BlockSpec(memory_space=pltpu.VMEM)] * 2
        + [pl.BlockSpec(memory_space=pltpu.HBM)] * 3,
        out_specs=[pl.BlockSpec(memory_space=pltpu.VMEM)] * 4,
        scratch_shapes=[pltpu.SemaphoreType.DMA((2, NX, 3))],
        compiler_params=pltpu.CompilerParams(vmem_limit_bytes=4 << 20),
        cost_estimate=pl.CostEstimate(
            flops=0, bytes_accessed=26 << 20, transcendentals=0
        ),
    )(infos, routing, gates, *weights)


def order(info, b, a):
    first = info[NX] == 0
    return jnp.where(first, b, a), jnp.where(first, a, b)


def load_rows(info, pieces, rows):
    step = rows.shape[2] // NY
    for b in range(4):
        for a in range(4):
            k, j = order(info, b, a)
            at = pl.ds(pl.multiple_of(j * step, step), step)
            for i in range(2):
                rows[k, i, at] = pieces[b][a, i]


def contract(rows, buf, acc):
    two = acc.shape[0] // 3 * 2

    @pl.loop(0, NX)
    def _(k):
        acc[:two] += lax.dot_general(
            buf[k, :two], rows[k, 0], NT, preferred_element_type=F32
        )
        acc[two:] += lax.dot_general(
            buf[k, two:], rows[k, 1], NT, preferred_element_type=F32
        )


def expand(info, hidden, grads, buf, out):
    step = hidden.shape[0] // NY
    two = grads.shape[1]

    def put(k, i, value):
        for j in range(NY):
            b, a = order(info, k, j)
            out[b, a, i] = value[j * step : (j + 1) * step]

    @pl.loop(0, NX)
    def _(k):
        o = jnp.dot(hidden[...], buf[k, two:], preferred_element_type=F32)
        put(k, 0, o.astype(BF))
        o = jnp.dot(grads[...], buf[k, :two], preferred_element_type=F32)
        put(k, 1, o.astype(BF))


def own_kernel(info, *refs):
    pieces, (buf, acc, rows) = refs[:4], refs[4:]
    load_rows(info, pieces, rows)
    acc[...] = jnp.zeros_like(acc)
    contract(rows, buf, acc)


def other_kernel(info, *refs):
    pieces, (buf, partial, out, hidden, grads, rows, acc) = refs[:4], refs[4:]
    load_rows(info, pieces, rows)
    acc[...] = partial[...]
    contract(rows, buf, acc)
    one = acc.shape[0] // 3
    g, u, h = acc[:one], acc[one : 2 * one], acc[2 * one :]
    sigma = jax.nn.sigmoid(g)
    hidden[...] = (g * sigma * u).T.astype(BF)
    gate_grad = h * u * sigma * (1.0 + g * (1.0 - sigma))
    grads[...] = jnp.concatenate([gate_grad, h * g * sigma], axis=0).T.astype(BF)
    expand(info, hidden, grads, buf, out)


def last_kernel(info, hidden, grads, buf, out):
    expand(info, hidden, grads, buf, out)


def call(body, name, info, arrays, out, scratch, products, shape):
    rows, hidden, width = shape
    return pl.pallas_call(
        body,
        name=name,
        out_shape=out,
        in_specs=[pl.BlockSpec(memory_space=pltpu.SMEM)]
        + [pl.BlockSpec(memory_space=pltpu.VMEM)] * len(arrays),
        out_specs=[pl.BlockSpec(memory_space=pltpu.VMEM)] * len(out),
        scratch_shapes=scratch,
        compiler_params=pltpu.CompilerParams(vmem_limit_bytes=VMEM_LIMIT[name] << 20),
        cost_estimate=pl.CostEstimate(
            flops=2 * products * rows * width * NX * hidden,
            bytes_accessed=7 << 20,
            transcendentals=0,
        ),
    )(info, *arrays)


def on_device(tokens, out_grad, gate_values, routing, gate_weight, up_weight, down_weight):
    width = tokens.shape[1]
    cut = lax.axis_index("cuts")
    x, c = cut // 2, cut % 2
    wg = jnp.swapaxes(gate_weight[0], 0, 1)
    wu = jnp.swapaxes(up_weight[0], 0, 1)
    w2 = down_weight[0]
    hidden = w2.shape[0]
    steps = jnp.arange(NX + 1)
    there = jnp.where(steps == 2, (x + 3 + 2 * (x % 2)) % NX, x ^ steps)
    there = jnp.where(steps == 3, x ^ 2, there)
    own_info = jnp.where(steps < NX, there * 2 + c, c)
    other_info = own_info ^ 1
    rows = NY * E * CAP

    turned = jnp.swapaxes(routing, 0, 1), jnp.swapaxes(gate_values, 0, 1)
    sources = tokens, out_grad, *turned
    send = pl.pallas_call(
        send_kernel,
        name="send",
        out_shape=jax.ShapeDtypeStruct((E, 2 * CAP, width), BF),
        in_specs=[pl.BlockSpec(memory_space=pl.ANY)] * 4,
        out_specs=pl.BlockSpec(memory_space=pltpu.VMEM),
        scratch_shapes=[pltpu.VMEM(v.shape, v.dtype) for v in sources]
        + [pltpu.SemaphoreType.DMA((4,))],
    )(*[pltpu.with_memory_space_constraint(v, pltpu.HBM) for v in sources])
    got = swap_z(send).reshape(E, 2, CAP, width)
    got = jnp.swapaxes(got, 0, 1).reshape(2, E * CAP, width)

    parts = gather(got, 0)
    token = to_core(parts[3][0, :8])[0]
    near = jnp.where(token == token, jnp.stack(parts), jnp.zeros((), BF))
    weights = [pltpu.with_memory_space_constraint(w, pltpu.HBM) for w in (wg, wu, w2)]
    infos, near = lax.optimization_barrier((jnp.stack([own_info, other_info]), near))
    bufs = load_weights(infos, *turned, weights, width)
    third, first, second = (swap(near, q, 1) for q in (3, 1, 2))
    other = tuple(to_core(v) for v in (near, first, second))
    third, other, bufs = lax.optimization_barrier((third, other, tuple(bufs)))
    other = [*other, to_core(third)]
    own = [near, first, second, third]

    pre = jax.ShapeDtypeStruct((3 * hidden, rows), F32)
    act = [
        jax.ShapeDtypeStruct((rows, hidden), BF),
        jax.ShapeDtypeStruct((rows, 2 * hidden), BF),
    ]
    pieces = [jax.ShapeDtypeStruct((4, 4, 2, rows // 4, width), BF)]
    row_buf = [pltpu.VMEM((NX, 2, rows, width), BF)]
    acc_buf = [pltpu.VMEM(pre.shape, F32)]
    shape = rows, hidden, width
    (partial,) = call(
        own_kernel, "own", own_info, [*own, bufs[0]], [pre], row_buf, 3, shape
    )
    far, *act = call(
        other_kernel, "other", other_info, [*other, bufs[1], partial],
        pieces + act, row_buf + acc_buf, 6, shape,
    )
    (near,) = call(
        last_kernel, "last", own_info, [*act, bufs[0]], pieces, [], 3, shape
    )
    got = to_core(far)
    sums = scatter([add(near[b], got[b]) for b in range(4)], 1)
    back = scatter([sums[a] for a in range(4)], 0)
    back = back.reshape(2, E, CAP, width)
    back = jnp.swapaxes(back, 0, 1).reshape(E, 2 * CAP, width)
    back = swap_z(back)
    result = [jax.ShapeDtypeStruct(tokens.shape, BF)] * 2
    return tuple(small(combine_kernel, "combine", result, [back, bufs[2], bufs[3]]))


def solution(mesh):
    return jax.shard_map(
        on_device,
        mesh=mesh,
        in_specs=(
            P("dp", "cuts"),
            P("dp", "cuts"),
            P("dp", None),
            P("dp", None),
            P("dp", None, "cuts"),
            P("dp", None, "cuts"),
            P("dp", "cuts", None),
        ),
        out_specs=(P("dp", "cuts"), P("dp", "cuts")),
        check_vma=False,
    )
```

```python
import itertools

import jax
import jax.numpy as jnp
from jax import lax
from jax.experimental import pallas as pl
from jax.experimental.pallas import tpu as pltpu
from jax.sharding import PartitionSpec as P

E = 8
NY = 4
NX = 4
CAP = 8
TOPK = 2
BF = jnp.bfloat16
F32 = jnp.float32
NT = (((1,), (1,)), ((), ()))
VMEM_LIMIT = {"own": 8, "other": 12, "last": 4}


Z_GROUPS = [[z * NY + y for z in reversed(range(E))] for y in range(NY)]


def swap_z(v):
    return lax.all_to_all(v, "dp", 0, 0, axis_index_groups=Z_GROUPS, tiled=True)


def partner(i, q):
    if q == 1:
        return i ^ 1
    return (i + (1 if i % 2 else 3)) % 4 if q == 2 else i ^ 2


def swap(v, q, along_y):
    def place(z, y, x, c):
        return (z * NY + y) * 2 * NX + x * 2 + c

    perm = []
    for z, y, x, c in itertools.product(range(E), range(NY), range(NX), range(2)):
        if c == along_y:
            to = place(z, partner(y, q), x, c)
        else:
            to = place(z, y, partner(x, q), c)
        perm.append((place(z, y, x, c), to))
    return lax.ppermute(v, ("dp", "cuts"), perm)


def to_core(v):
    return lax.ppermute(v, "cuts", [(i, i ^ 1) for i in range(2 * NX)])


def thirds(v):
    first = v.astype(BF)
    rest = v - first.astype(F32)
    second = rest.astype(BF)
    return first, second, (rest - second.astype(F32)).astype(BF)


def later(n):
    i = lax.broadcasted_iota(jnp.int32, (n, n), 0)
    j = lax.broadcasted_iota(jnp.int32, (n, n), 1)
    return jnp.where(i < j, 1.0, 0.0).astype(BF)


def choose(routing, gates):
    shape = E * CAP, routing.shape[1]
    index = lax.broadcasted_iota(jnp.int32, shape, 0)
    expert = index // CAP
    is0 = routing[0:1, :] == expert
    chosen = is0 | (routing[1:2, :] == expert)
    flags = jnp.where(chosen, 1.0, 0.0).astype(BF)
    position = jnp.dot(flags, later(shape[1]), preferred_element_type=F32)
    select = chosen & (position == (index % CAP).astype(F32))
    return select, jnp.where(is0, gates[0:1, :], gates[1:2, :])


def send_kernel(tokens_in, dy_in, routing_in, gates_in, out, tokens, dy, routing, gates, sem):
    pairs = (routing_in, routing), (gates_in, gates), (tokens_in, tokens), (dy_in, dy)
    copies = [
        pltpu.make_async_copy(a, b, sem.at[n]) for n, (a, b) in enumerate(pairs)
    ]
    for copy in copies:
        copy.start()
    copies[0].wait()
    copies[1].wait()
    select, gate = choose(routing, gates)
    gate = jnp.sum(jnp.where(select, gate, 0.0), axis=1, keepdims=True)
    pick = jnp.where(select, 1.0, 0.0).astype(BF)
    copies[2].wait()
    copies[3].wait()
    x = jnp.dot(pick, tokens[...], preferred_element_type=F32)
    grad = gate * jnp.dot(pick, dy[...], preferred_element_type=F32)
    for e in range(E):
        at = slice(e * CAP, (e + 1) * CAP)
        out[E - 1 - e] = jnp.concatenate([x[at], grad[at]], axis=0).astype(BF)


def own_slots(routing, gates, mix, select_ref):
    rows = routing.shape[1]
    select, gate = choose(routing, gates)
    i = lax.broadcasted_iota(jnp.int32, (rows, rows), 0)
    j = lax.broadcasted_iota(jnp.int32, (rows, rows), 1)
    eye = jnp.where(i == j, 1.0, 0.0).astype(BF)

    def turned(v):
        return lax.dot_general(eye, v, NT, preferred_element_type=F32).astype(BF)

    select_ref[...] = turned(jnp.where(select, 1.0, 0.0).astype(BF))
    for n, part in enumerate(thirds(jnp.where(select, gate, 0.0))):
        mix[n] = turned(part)


def combine_kernel(back, mix, select, mixed, grad):
    def rows(at):
        parts = [back[E - 1 - e, at : at + CAP].astype(F32) for e in range(E)]
        return jnp.concatenate(parts, axis=0).astype(BF)

    y, dx = rows(0), rows(CAP)
    total = jnp.dot(mix[0], y, preferred_element_type=F32)
    for n in (1, 2):
        total = total + jnp.dot(mix[n], y, preferred_element_type=F32)
    mixed[...] = total.astype(BF)
    grad[...] = jnp.dot(select[...], dx, preferred_element_type=F32).astype(BF)


def small(body, name, out, arrays, scalars=0):
    return pl.pallas_call(
        body,
        name=name,
        out_shape=out,
        in_specs=[pl.BlockSpec(memory_space=pltpu.SMEM)] * scalars
        + [pl.BlockSpec(memory_space=pltpu.VMEM)] * (len(arrays) - scalars),
        out_specs=jax.tree.map(lambda _: pl.BlockSpec(memory_space=pltpu.VMEM), out),
        compiler_params=pltpu.CompilerParams(vmem_limit_bytes=4 << 20),
    )(*arrays)


def gather(v, along_y):
    next_, near, far = lax.optimization_barrier(
        tuple(swap(v, q, along_y) for q in (2, 1, 3))
    )
    return [v, near, next_, far]


def add(*parts):
    total = parts[0].astype(F32)
    for p in parts[1:]:
        total = total + p.astype(F32)
    return total.astype(BF)


def scatter(parts, along_y):
    parts = lax.optimization_barrier(tuple(parts))
    got = lax.optimization_barrier(
        tuple(swap(parts[q], q, along_y) for q in (3, 1, 2))
    )
    return add(parts[0], *got)


def weights_kernel(infos, routing, gates, *refs):
    weights, bufs, mix, select, sem = refs[:3], refs[3:5], refs[5], refs[6], refs[7]
    hidden, width = weights[0].shape[0], bufs[0].shape[-1]
    copies = []
    for core in range(2):
        for k in range(NX):
            at = pl.ds(pl.multiple_of(infos[core, k] * width, 128), width)
            for i in range(3):
                to = bufs[core].at[k, pl.ds(i * hidden, hidden)]
                copies.append(
                    pltpu.make_async_copy(
                        weights[i].at[:, at], to, sem.at[core, k, i]
                    )
                )
    for copy in copies:
        copy.start()
    own_slots(routing, gates, mix, select)
    for copy in copies:
        copy.wait()


def load_weights(infos, routing, gates, weights, width):
    hidden = weights[0].shape[0]
    return pl.pallas_call(
        weights_kernel,
        name="weights",
        out_shape=[jax.ShapeDtypeStruct((NX, 3 * hidden, width), BF)] * 2
        + [
            jax.ShapeDtypeStruct((3, routing.shape[1], E * CAP), BF),
            jax.ShapeDtypeStruct((routing.shape[1], E * CAP), BF),
        ],
        in_specs=[pl.BlockSpec(memory_space=pltpu.SMEM)]
        + [pl.BlockSpec(memory_space=pltpu.VMEM)] * 2
        + [pl.BlockSpec(memory_space=pltpu.HBM)] * 3,
        out_specs=[pl.BlockSpec(memory_space=pltpu.VMEM)] * 4,
        scratch_shapes=[pltpu.SemaphoreType.DMA((2, NX, 3))],
        compiler_params=pltpu.CompilerParams(vmem_limit_bytes=4 << 20),
        cost_estimate=pl.CostEstimate(
            flops=0, bytes_accessed=26 << 20, transcendentals=0
        ),
    )(infos, routing, gates, *weights)


def order(info, b, a):
    first = info[NX] == 0
    return jnp.where(first, b, a), jnp.where(first, a, b)


def load_rows(info, pieces, rows):
    step = rows.shape[2] // NY
    for b in range(4):
        for a in range(4):
            k, j = order(info, b, a)
            at = pl.ds(pl.multiple_of(j * step, step), step)
            for i in range(2):
                rows[k, i, at] = pieces[b][a, i]


def contract(rows, buf, acc):
    two = acc.shape[0] // 3 * 2

    @pl.loop(0, NX)
    def _(k):
        acc[:two] += lax.dot_general(
            buf[k, :two], rows[k, 0], NT, preferred_element_type=F32
        )
        acc[two:] += lax.dot_general(
            buf[k, two:], rows[k, 1], NT, preferred_element_type=F32
        )


def expand(info, hidden, grads, buf, out):
    step = hidden.shape[0] // NY
    two = grads.shape[1]

    def put(k, i, value):
        for j in range(NY):
            b, a = order(info, k, j)
            out[b, a, i] = value[j * step : (j + 1) * step]

    @pl.loop(0, NX)
    def _(k):
        o = jnp.dot(hidden[...], buf[k, two:], preferred_element_type=F32)
        put(k, 0, o.astype(BF))
        o = jnp.dot(grads[...], buf[k, :two], preferred_element_type=F32)
        put(k, 1, o.astype(BF))


def own_kernel(info, *refs):
    pieces, (buf, acc, rows) = refs[:4], refs[4:]
    load_rows(info, pieces, rows)
    acc[...] = jnp.zeros_like(acc)
    contract(rows, buf, acc)


def other_kernel(info, *refs):
    pieces, (buf, partial, out, hidden, grads, rows, acc) = refs[:4], refs[4:]
    load_rows(info, pieces, rows)
    acc[...] = partial[...]
    contract(rows, buf, acc)
    one = acc.shape[0] // 3
    g, u, h = acc[:one], acc[one : 2 * one], acc[2 * one :]
    sigma = jax.nn.sigmoid(g)
    hidden[...] = (g * sigma * u).T.astype(BF)
    gate_grad = h * u * sigma * (1.0 + g * (1.0 - sigma))
    grads[...] = jnp.concatenate([gate_grad, h * g * sigma], axis=0).T.astype(BF)
    expand(info, hidden, grads, buf, out)


def last_kernel(info, hidden, grads, buf, out):
    expand(info, hidden, grads, buf, out)


def call(body, name, info, arrays, out, scratch, products, shape):
    rows, hidden, width = shape
    return pl.pallas_call(
        body,
        name=name,
        out_shape=out,
        in_specs=[pl.BlockSpec(memory_space=pltpu.SMEM)]
        + [pl.BlockSpec(memory_space=pltpu.VMEM)] * len(arrays),
        out_specs=[pl.BlockSpec(memory_space=pltpu.VMEM)] * len(out),
        scratch_shapes=scratch,
        compiler_params=pltpu.CompilerParams(vmem_limit_bytes=VMEM_LIMIT[name] << 20),
        cost_estimate=pl.CostEstimate(
            flops=2 * products * rows * width * NX * hidden,
            bytes_accessed=7 << 20,
            transcendentals=0,
        ),
    )(info, *arrays)


def on_device(tokens, out_grad, gate_values, routing, gate_weight, up_weight, down_weight):
    width = tokens.shape[1]
    cut = lax.axis_index("cuts")
    x, c = cut // 2, cut % 2
    wg = jnp.swapaxes(gate_weight[0], 0, 1)
    wu = jnp.swapaxes(up_weight[0], 0, 1)
    w2 = down_weight[0]
    hidden = w2.shape[0]
    steps = jnp.arange(NX + 1)
    there = jnp.where(steps == 2, (x + 3 + 2 * (x % 2)) % NX, x ^ steps)
    there = jnp.where(steps == 3, x ^ 2, there)
    own_info = jnp.where(steps < NX, there * 2 + c, c)
    other_info = own_info ^ 1
    rows = NY * E * CAP

    turned = jnp.swapaxes(routing, 0, 1), jnp.swapaxes(gate_values, 0, 1)
    sources = tokens, out_grad, *turned
    send = pl.pallas_call(
        send_kernel,
        name="send",
        out_shape=jax.ShapeDtypeStruct((E, 2 * CAP, width), BF),
        in_specs=[pl.BlockSpec(memory_space=pl.ANY)] * 4,
        out_specs=pl.BlockSpec(memory_space=pltpu.VMEM),
        scratch_shapes=[pltpu.VMEM(v.shape, v.dtype) for v in sources]
        + [pltpu.SemaphoreType.DMA((4,))],
    )(*[pltpu.with_memory_space_constraint(v, pltpu.HBM) for v in sources])
    got = swap_z(send).reshape(E, 2, CAP, width)
    got = jnp.swapaxes(got, 0, 1).reshape(2, E * CAP, width)

    parts = gather(got, 0)
    token = to_core(parts[3][0, :8])[0]
    near = jnp.where(token == token, jnp.stack(parts), jnp.zeros((), BF))
    weights = [pltpu.with_memory_space_constraint(w, pltpu.HBM) for w in (wg, wu, w2)]
    infos, near = lax.optimization_barrier((jnp.stack([own_info, other_info]), near))
    bufs = load_weights(infos, *turned, weights, width)
    third, first, second = (swap(near, q, 1) for q in (3, 1, 2))
    other = tuple(to_core(v) for v in (near, first, second))
    third, other, bufs = lax.optimization_barrier((third, other, tuple(bufs)))
    other = [*other, to_core(third)]
    own = [near, first, second, third]

    pre = jax.ShapeDtypeStruct((3 * hidden, rows), F32)
    act = [
        jax.ShapeDtypeStruct((rows, hidden), BF),
        jax.ShapeDtypeStruct((rows, 2 * hidden), BF),
    ]
    pieces = [jax.ShapeDtypeStruct((4, 4, 2, rows // 4, width), BF)]
    row_buf = [pltpu.VMEM((NX, 2, rows, width), BF)]
    acc_buf = [pltpu.VMEM(pre.shape, F32)]
    shape = rows, hidden, width
    (partial,) = call(
        own_kernel, "own", own_info, [*own, bufs[0]], [pre], row_buf, 3, shape
    )
    far, *act = call(
        other_kernel, "other", other_info, [*other, bufs[1], partial],
        pieces + act, row_buf + acc_buf, 6, shape,
    )
    (near,) = call(
        last_kernel, "last", own_info, [*act, bufs[0]], pieces, [], 3, shape
    )
    got = to_core(far)
    sums = scatter([add(near[b], got[b]) for b in range(4)], 1)
    back = scatter([sums[a] for a in range(4)], 0)
    back = back.reshape(2, E, CAP, width)
    back = jnp.swapaxes(back, 0, 1).reshape(E, 2 * CAP, width)
    back = swap_z(back)
    result = [jax.ShapeDtypeStruct(tokens.shape, BF)] * 2
    return tuple(small(combine_kernel, "combine", result, [back, bufs[2], bufs[3]]))


def solution(mesh):
    return jax.shard_map(
        on_device,
        mesh=mesh,
        in_specs=(
            P("dp", "cuts"),
            P("dp", "cuts"),
            P("dp", None),
            P("dp", None),
            P("dp", None, "cuts"),
            P("dp", None, "cuts"),
            P("dp", "cuts", None),
        ),
        out_specs=(P("dp", "cuts"), P("dp", "cuts")),
        check_vma=False,
    )
```
